32 devices in a mesh: dp: 16 (over z, y, x), mp: 2 (over core).
Axes of the slice: x: 2, y: 2, z: 4, core: 2. Of those that a mesh axis runs over, the one named last changes fastest.
Arguments:
- tokens: bfloat16 [32768, 768], P(('dp', 'mp')), may hold values from -6 to 6
- w_query: bfloat16 [768, 768], P('dp', 'mp'), may hold values from -0.21875 to 0.21875
- w_key: bfloat16 [768, 768], P('dp', 'mp'), may hold values from -0.21875 to 0.21875
- w_value: bfloat16 [768, 768], P('dp', 'mp'), may hold values from -0.21875 to 0.21875
- w_out: bfloat16 [768, 768], P('mp', 'dp'), may hold values from -0.875 to 0.875
- w_gate: bfloat16 [768, 3072], P('dp', 'mp'), may hold values from -0.21875 to 0.21875
- w_up: bfloat16 [768, 3072], P('dp', 'mp'), may hold values from -0.21875 to 0.21875
- w_down: bfloat16 [3072, 768], P('mp', 'dp'), may hold values from -0.109375 to 0.109375
- attention_norm_gain: float32 [768], replicated, may hold values from 0.5 to 1.5
- feedforward_norm_gain: float32 [768], replicated, may hold values from 0.5 to 1.5
- block_seq: int32 [16, 32], P('dp'), may hold values from 0 to 31, as said below
- block_len: int32 [16, 32], P('dp'), may hold values from 0 to 64, as said below
- cotangent: bfloat16 [32768, 768], P(('dp', 'mp')), may hold values from -6 to 6
Outputs:
- output: bfloat16 [32768, 768], P(('dp', 'mp'))
- input_grad: bfloat16 [32768, 768], P(('dp', 'mp'))
- grad_w_query: float32 [768, 768], P('dp', 'mp')
- grad_w_key: float32 [768, 768], P('dp', 'mp')
- grad_w_value: float32 [768, 768], P('dp', 'mp')
- grad_w_out: float32 [768, 768], P('mp', 'dp')
- grad_w_gate: float32 [768, 3072], P('dp', 'mp')
- grad_w_up: float32 [768, 3072], P('dp', 'mp')
- grad_w_down: float32 [3072, 768], P('mp', 'dp')
- grad_gain_attn: float32 [768], replicated
- grad_gain_ffn: float32 [768], replicated
The draws below stay inside these ranges and needn't reach their ends.
Inputs may be any that keep to these rules, and one draw needn't show every extreme that they name: `block_seq`: within each pack (aligned runs of 32 entries of a row) either every entry is 0, one document, or entry b of the pack is b, one query to a block; in every draw some pack holds a document and some pack holds queries. `block_len`: A query holds 8 to 64 valid rows, and one query of every query pack holds 64. A document of L rows, 64 <= L <= 2048, has 64 valid rows in its blocks before row L - L % 64, L % 64 in the next block and 0 after; in every draw some document holds 2048 rows.
All inputs are finite; a program needn't handle non-finite values.
Results may differ from the reference program's by a relative error of at most 0.02.
Values may be sent and summed in bfloat16 or wider, within the bound.
No kernel may reach another device: no remote copies, remote signals or barrier semaphores. Data moves between devices by JAX's collectives and lax.ppermute only.
A program may use at most 256 MiB of HBM per device.

```python
import math
import jax
import jax.numpy as jnp
from jax import lax

D = 768
FF = 3072
HEAD_DIM = 64
SEQ_MAX = 2048
QLEN = 64
PACKS = 1
HEADS = 12
TOKENS = 32768
N_DP = 16


def pack_layout(key):
    base = jax.random.fold_in(key, 7)
    streams = jax.random.split(base, 6)
    packs = N_DP * PACKS
    blocks = SEQ_MAX // QLEN
    index = jnp.arange(packs, dtype=jnp.int32)
    doc_pick = jax.random.randint(streams[0], (), 0, packs)
    query_pick = (doc_pick + 1 + jax.random.randint(streams[1], (), 0, packs - 1)) % packs
    is_doc = jax.random.randint(streams[2], (packs,), 0, 2)
    is_doc = jnp.where(index == doc_pick, 1, jnp.where(index == query_pick, 0, is_doc))
    doc_len = jax.random.randint(streams[3], (packs,), QLEN, SEQ_MAX + 1)
    doc_len = jnp.where(index == doc_pick, SEQ_MAX, doc_len)
    query_len = jax.random.randint(streams[4], (packs, blocks), QLEN // 8, QLEN + 1)
    slot = jax.random.randint(streams[5], (packs,), 0, blocks)
    block = jnp.arange(blocks, dtype=jnp.int32)
    query_len = jnp.where(block[None, :] == slot[:, None], QLEN, query_len)
    doc_blocks = jnp.clip(doc_len[:, None] - block[None, :] * QLEN, 0, QLEN)
    lengths = jnp.where(is_doc[:, None] == 1, doc_blocks, query_len)
    sequence = jnp.where(is_doc[:, None] == 1, 0, block[None, :] + 0 * query_len)
    return (sequence.reshape(N_DP, PACKS * blocks).astype(jnp.int32), lengths.reshape(N_DP, PACKS * blocks).astype(jnp.int32))


def draw_block_seq(key, part):
    return pack_layout(key)[0]


def draw_block_len(key, part):
    return pack_layout(key)[1]


def raised(values, rng, source, target, shards_of, factor):
    owner, partner = [(jnp.arange(values.shape[axis_at]) // (values.shape[axis_at] // shards_of)).reshape([-1 if axis == axis_at else 1 for axis in range(values.ndim)]) for axis_at in (source, target)]
    chosen = jax.random.permutation(rng, shards_of)[partner]
    strong = (owner == chosen) | (owner == (partner + shards_of // 2) % shards_of)
    return jnp.where(strong, factor * values, values)


def block_levels(rng, extent, pieces, low, largest):
    def one(dim, blocks):
        draws = jax.random.uniform(jax.random.fold_in(jax.random.fold_in(rng, 6), dim), (blocks,), jnp.float32, low / len(pieces), largest / len(pieces))
        return jnp.repeat(jnp.exp(draws), extent[dim] // blocks).reshape((-1,) + (1,) * (len(extent) - dim - 1))

    level = one(*pieces[0])
    for cut in pieces[1:]:
        level = level * one(*cut)
    return level


def bell_draw(stream_key, shape, scale, limit, cuts=(), kind=jnp.bfloat16):
    entries = jax.random.normal(stream_key, shape, jnp.float32) * scale
    if len(cuts) > 0:
        entries = block_levels(stream_key, shape, cuts, -0.22, 0.18) * entries
    return jnp.clip(entries, min=-limit, max=limit).astype(kind)


def heavy_noise(own_key, shape, deviation, limit, cuts, heavy, held_as=jnp.bfloat16):
    drawn = deviation * jax.random.normal(own_key, shape, jnp.float32)
    if cuts:
        drawn = drawn * block_levels(own_key, shape, cuts, -0.22, 0.18)
    return jnp.clip(raised(drawn, jax.random.fold_in(own_key, 3), *heavy), -limit, limit).astype(held_as)


def setup_inputs(seed: int = 0) -> dict:
    key_list = jax.random.split(jax.random.key(seed), 14)
    return {
        "tokens": heavy_noise(key_list[0], (TOKENS, D), 1.0, 6.0, ((0, 32),), (0, 1, 32, 2.75)),
        "w_query": bell_draw(key_list[1], (D, D), D ** -0.5, 0.21875, ((0, 16), (1, 2))),
        "w_key": bell_draw(key_list[2], (D, D), D ** -0.5, 0.21875, ((0, 16), (1, 2))),
        "w_value": bell_draw(key_list[3], (D, D), D ** -0.5, 0.21875, ((0, 16), (1, 2))),
        "w_out": bell_draw(key_list[4], (D, D), (D // 16) ** -0.5, 0.875, ((0, 2), (1, 16))),
        "w_gate": bell_draw(key_list[5], (D, FF), D ** -0.5, 0.21875, ((0, 16), (1, 2))),
        "w_up": bell_draw(key_list[6], (D, FF), D ** -0.5, 0.21875, ((0, 16), (1, 2))),
        "w_down": bell_draw(key_list[7], (FF, D), FF ** -0.5, 0.109375, ((0, 2), (1, 16))),
        "attention_norm_gain": jnp.clip(1.0 + 0.1 * jax.random.normal(key_list[8], (D,), jnp.float32), 0.5, 1.5),
        "feedforward_norm_gain": jnp.clip(1.0 + 0.1 * jax.random.normal(key_list[9], (D,), jnp.float32), 0.5, 1.5),
        "block_seq": draw_block_seq(jax.random.fold_in(key_list[13], 71), 0),
        "block_len": draw_block_len(jax.random.fold_in(key_list[13], 71), 0),
        "cotangent": heavy_noise(key_list[12], (TOKENS, D), 1.0, 6.0, ((0, 32),), (0, 1, 32, 2.75)),
    }


EPS = 1e-05
ROPE_BASE = 1000.0
HIGHEST = lax.Precision.HIGHEST

@jax.custom_vjp
def low(v):
    return lax.optimization_barrier(v.astype(jnp.bfloat16)).astype(jnp.float32)

@jax.custom_vjp
def low_back(v):
    return v

def low_keep(v):
    return (low(v), None)

def low_pass(kept, upstream_gradient):
    return (upstream_gradient,)

def back_keep(v):
    return (v, None)

def back_low(kept, upstream_gradient):
    return (low(upstream_gradient),)
low.defvjp(low_keep, low_pass)
low_back.defvjp(back_keep, back_low)

def block_layout(seq_row, len_row):
    blocks = SEQ_MAX // QLEN
    sequence = seq_row.reshape(PACKS, blocks)
    lengths = len_row.reshape(PACKS, blocks)
    earlier = lax.optimization_barrier(jnp.sum((sequence[:, None, :] < sequence[:, :, None]).astype(jnp.int32), axis=2))
    inside = jnp.arange(SEQ_MAX, dtype=jnp.int32)
    row_seq = jnp.repeat(sequence, QLEN, axis=1)
    position = inside[None, :] - QLEN * jnp.repeat(earlier, QLEN, axis=1)
    key_valid = (inside % QLEN)[None, :] < jnp.repeat(lengths, QLEN, axis=1)
    return (row_seq, position, key_valid)

def rotary_tables(position):
    half = HEAD_DIM // 2
    ladder = jnp.arange(half, dtype=jnp.int32).astype(jnp.float32)
    inverse = jnp.exp(ladder * (-2.0 * math.log(ROPE_BASE) / HEAD_DIM))
    angle = position.astype(jnp.float32)[:, None] * inverse[None, :]
    return (jnp.cos(angle), jnp.sin(angle))

def rotate(value, cosine, sine):
    half = value.shape[-1] // 2
    first = value[..., :half]
    second = value[..., half:]
    cos_row = cosine[:, None, :]
    sin_row = sine[:, None, :]
    return jnp.concatenate([first * cos_row - second * sin_row, second * cos_row + first * sin_row], axis=-1)

def norm(value, norm_gain):
    row_mean = lax.optimization_barrier(jnp.mean(value, axis=-1, keepdims=True))
    centred = value - row_mean
    spread = lax.optimization_barrier(jnp.mean(centred * centred, axis=-1, keepdims=True))
    return centred * lax.rsqrt(spread + EPS) * norm_gain

def attend_block(query_block, keys, values, row_seq, key_seq, key_valid):
    scores = jnp.einsum('qhd,khd->hqk', query_block, keys, precision=HIGHEST) * HEAD_DIM ** (-0.5)
    scores = low_back(scores)
    allowed = (row_seq[:, None] == key_seq[None, :]) & key_valid[None, :]
    scores = jnp.where(allowed[None], scores, -1e+30)
    peak = lax.optimization_barrier(jnp.max(scores, axis=-1, keepdims=True))
    expo = jnp.exp(scores - peak)
    probs = low(expo / lax.optimization_barrier(jnp.sum(expo, axis=-1, keepdims=True)))
    return jnp.einsum('hqk,khd->qhd', probs, values, precision=HIGHEST)

def group_layer(tokens, w_query, w_key, w_value, w_out, w_gate, w_up, w_down, attention_norm_gain, feedforward_norm_gain, row_seq, position, key_valid):
    rows = tokens.shape[0]
    cosine, sine = rotary_tables(position.reshape(rows))
    query = low(rotate(low_back(jnp.dot(tokens, w_query, precision=HIGHEST)).reshape(rows, HEADS, HEAD_DIM), cosine, sine))
    keys = low(rotate(low_back(jnp.dot(tokens, w_key, precision=HIGHEST)).reshape(rows, HEADS, HEAD_DIM), cosine, sine))
    values = low(low_back(jnp.dot(tokens, w_value, precision=HIGHEST))).reshape(rows, HEADS, HEAD_DIM)
    block = min(512, SEQ_MAX)
    count = SEQ_MAX // block
    step = jax.checkpoint(attend_block)

    def one_pack(item):
        query_pack, key_pack, value_pack, seq_pack, valid_pack = item

        def one_block(piece):
            query_block, seq_block = piece
            return step(query_block, key_pack, value_pack, seq_block, seq_pack, valid_pack)
        mixed = lax.map(one_block, (query_pack.reshape(count, block, HEADS, HEAD_DIM), seq_pack.reshape(count, block)))
        return mixed.reshape(SEQ_MAX, HEADS, HEAD_DIM)
    mixed = lax.map(one_pack, (query.reshape(PACKS, SEQ_MAX, HEADS, HEAD_DIM), keys.reshape(PACKS, SEQ_MAX, HEADS, HEAD_DIM), values.reshape(PACKS, SEQ_MAX, HEADS, HEAD_DIM), row_seq, key_valid))
    context = low(low_back(mixed.reshape(rows, D)))
    attention_output = low_back(jnp.dot(context, w_out, precision=HIGHEST))
    hidden_state = norm(tokens + attention_output, attention_norm_gain)
    hidden_low = low(hidden_state)
    gate = low_back(jnp.dot(hidden_low, w_gate, precision=HIGHEST))
    up_value = low_back(jnp.dot(hidden_low, w_up, precision=HIGHEST))
    act = low(gate * jax.nn.sigmoid(gate) * up_value)
    branch_output = low_back(jnp.dot(act, w_down, precision=HIGHEST))
    return norm(hidden_state + branch_output, feedforward_norm_gain)

def reference(tokens, w_query, w_key, w_value, w_out, w_gate, w_up, w_down, attention_norm_gain, feedforward_norm_gain, block_seq, block_len, cotangent):
    rows = PACKS * SEQ_MAX
    weights = tuple((w.astype(jnp.float32) for w in (w_query, w_key, w_value, w_out, w_gate, w_up, w_down, attention_norm_gain, feedforward_norm_gain)))
    inputs = tokens.astype(jnp.float32).reshape(N_DP, rows, D)
    cotangents = cotangent.astype(jnp.float32).reshape(N_DP, rows, D)

    def group(totals, item):
        group_in, group_cot, seq_row, len_row = item
        row_seq, position, key_valid = block_layout(seq_row, len_row)

        def forward(value, wq_in, wk_in, wv_in, wo_in, wg_in, wu_in, wd_in, ga_in, gf_in):
            return group_layer(value, wq_in, wk_in, wv_in, wo_in, wg_in, wu_in, wd_in, ga_in, gf_in, row_seq, position, key_valid)
        result, pullback = jax.vjp(forward, group_in, weights[0], weights[1], weights[2], weights[3], weights[4], weights[5], weights[6], weights[7], weights[8])
        grads = pullback(group_cot)
        totals = tuple((total + upstream_gradient for total, upstream_gradient in zip(totals, grads[1:])))
        return (totals, (result.astype(jnp.bfloat16), grads[0].astype(jnp.bfloat16)))
    zeros = tuple((jnp.zeros(w.shape, jnp.float32) for w in weights))
    totals, (outputs, input_grads) = lax.scan(group, zeros, (inputs, cotangents, block_seq, block_len))
    return (outputs.reshape(TOKENS, D), input_grads.reshape(TOKENS, D), totals[0], totals[1], totals[2], totals[3], totals[4], totals[5], totals[6], totals[7], totals[8])
```

```python
import functools
import math

import jax
import jax.numpy as jnp
from jax import lax
from jax.experimental import pallas as pl
from jax.experimental.pallas import tpu as pltpu
from jax.sharding import Mesh
from jax.sharding import PartitionSpec as P

HEAD_DIM = 64
SEQ_MAX = 2048
QLEN = 64
EPS = 1e-05
ROPE_BASE = 1000.0
MASKED = -1e30
SLOT = 128

bf16 = jnp.bfloat16
f32 = jnp.float32

NN = (((1,), (0,)), ((), ()))
NT = (((1,), (1,)), ((), ()))


def dot(left, right, dims=NN):
    return lax.dot_general(left, right, dims, preferred_element_type=f32)


def call(kernel, name, grid, in_specs, out_specs, out_shape, flops, scratch=(), aliases=None, exps=0):
    def run(*operands):
        outs = out_shape if isinstance(out_shape, (list, tuple)) else [out_shape]
        moved = sum(math.prod(o.shape) * o.dtype.itemsize for o in (*operands, *outs))
        return pl.pallas_call(
            kernel,
            name=name,
            grid=grid,
            in_specs=in_specs,
            out_specs=out_specs,
            out_shape=out_shape,
            scratch_shapes=list(scratch),
            input_output_aliases=aliases or {},
            cost_estimate=pl.CostEstimate(
                flops=int(flops), bytes_accessed=int(moved), transcendentals=int(exps)
            ),
            compiler_params=pltpu.CompilerParams(vmem_limit_bytes=60 * 1024 * 1024),
        )(*operands)

    return run


def shape(dims, dtype):
    return jax.ShapeDtypeStruct(dims, dtype)


def whole(dims):
    return pl.BlockSpec(dims, lambda *_: (0,) * len(dims))


def rope(value, cosine, sine, lane):
    half = HEAD_DIM // 2
    lanes = value.shape[-1]
    swapped = jnp.where(
        lane % HEAD_DIM < half,
        pltpu.roll(value, lanes - half, 1),
        pltpu.roll(value, half, 1),
    )
    return value * cosine + swapped * sine


def qkv_kernel(own_blocks, own_ref, par_ref, w_ref, cos_ref, sin_ref, eq_ref, ek_ref, q_ref, k_ref, v_ref):
    rows = jnp.where(pl.program_id(0) < own_blocks, own_ref[...], par_ref[...])
    lane = lax.broadcasted_iota(jnp.int32, (rows.shape[0], SLOT), 1)
    low = lane < HEAD_DIM
    ones = jnp.where((lane >= HEAD_DIM) & (lane < HEAD_DIM + 3), -1.0, 0.0)
    cosine, sine = cos_ref[...], sin_ref[...]
    ext_q, ext_k = eq_ref[...].astype(f32), ek_ref[...].astype(f32)
    for pair in range(q_ref.shape[0] // 2):
        base = pair * 3 * SLOT
        mixed = dot(rows, w_ref[:, base : base + 3 * SLOT])
        query = rope(mixed[:, :SLOT], cosine, sine, lane) * HEAD_DIM**-0.5
        key = rope(mixed[:, SLOT : 2 * SLOT], cosine, sine, lane)
        value = mixed[:, 2 * SLOT :]
        for ref, data, ext in ((q_ref, query, ext_q), (k_ref, key, ext_k), (v_ref, value, ones)):
            ref[2 * pair] = jnp.where(low, data, ext).astype(bf16)
            ref[2 * pair + 1] = jnp.where(low, pltpu.roll(data, HEAD_DIM, 1), ext).astype(bf16)


def project_qkv(own, par, weights, cosine, sine, ext_q, ext_k, block=256):
    rows, width = own.shape
    heads = weights.shape[1] // (3 * HEAD_DIM)
    count = rows // block
    table = pl.BlockSpec((block, SLOT), lambda i: (i, 0))
    out = pl.BlockSpec((heads, block, SLOT), lambda i: (0, i, 0))
    return call(
        functools.partial(qkv_kernel, count),
        "project_qkv",
        (2 * count,),
        [
            pl.BlockSpec((block, width), lambda i: (jnp.minimum(i, count - 1), 0)),
            pl.BlockSpec((block, width), lambda i: (jnp.maximum(i - count, 0), 0)),
            whole(weights.shape),
            table,
            table,
            table,
            table,
        ],
        [out] * 3,
        [shape((heads, 2 * rows, SLOT), bf16)] * 3,
        4 * rows * width * weights.shape[1],
    )(own, par, weights, cosine, sine, ext_q, ext_k)


def split_three(value):
    first = value.astype(bf16).astype(f32)
    second = (value - first).astype(bf16).astype(f32)
    return first, second, value - first - second


def attend_kernel(block, q_ref, k_ref, v_ref, ctx_ref, mix_ref, q2_ref):
    lane = lax.broadcasted_iota(jnp.int32, (block, SLOT), 1)
    low = lane < HEAD_DIM
    for piece in range(q_ref.shape[1] // block):
        rows = pl.ds(piece * block, block)
        mixed = []
        for head in range(2):
            query = q_ref[head, rows, :]
            scores = dot(query, k_ref[head], NT)
            peak = jnp.max(scores, axis=-1, keepdims=True)
            expo = jnp.exp(scores - peak).astype(bf16)
            total_mix = dot(expo, v_ref[head])
            total = -total_mix[:, HEAD_DIM : HEAD_DIM + 1]
            mixed.append(total_mix * (1.0 / total))
            parts = split_three(peak + jnp.log(total))
            kept = query.astype(f32)
            for at, part in enumerate(parts):
                kept = jnp.where(lane == HEAD_DIM + 32 + at, part, kept)
            q2_ref[head, rows, :] = kept.astype(bf16)
        both = jnp.where(low, mixed[0], pltpu.roll(mixed[1], HEAD_DIM, 1))
        mix_ref[rows, :] = both
        ctx_ref[rows, :] = both.astype(bf16)


def attend(query, keys, values, block=256, step=512):
    heads, rows, _ = query.shape
    piece = pl.BlockSpec((2, step, SLOT), lambda p, i: (p, i, 0))
    full = pl.BlockSpec((2, rows, SLOT), lambda p, i: (p, 0, 0))
    out = pl.BlockSpec((step, SLOT), lambda p, i: (i, p))
    width = heads * HEAD_DIM
    return call(
        functools.partial(attend_kernel, block),
        "attend",
        (heads // 2, rows // step),
        [piece, full, full],
        [out, out, piece],
        [shape((rows, width), bf16), shape((rows, width), f32), shape(query.shape, bf16)],
        4 * heads * rows * rows * SLOT,
        exps=heads * rows * rows,
    )(query, keys, values)


def attend_back_kernel(
    block, q_ref, k_ref, v_ref, own_ref, par_ref, mix_ref, cos_ref, sin_ref, out_ref, g_ref, acc_ref
):
    at = pl.program_id(0)
    rows = q_ref.shape[1]
    half = own_ref.shape[0]
    lane = lax.broadcasted_iota(jnp.int32, (half, SLOT), 1)
    low = lane < HEAD_DIM

    @pl.when(at == 0)
    def _():
        acc_ref[...] = jnp.zeros_like(acc_ref)
        for part, grad_ref in enumerate((own_ref, par_ref)):
            span = pl.ds(part * half, half)
            grad = grad_ref[...].astype(f32)
            product = grad * mix_ref[span, :]
            for head in range(2):
                mine = low if head == 0 else ~low
                delta = jnp.sum(jnp.where(mine, product, 0.0), axis=-1, keepdims=True)
                kept = grad if head == 0 else pltpu.roll(grad, HEAD_DIM, 1)
                kept = jnp.where(low, kept, 0.0)
                for n, piece in enumerate(split_three(delta)):
                    kept = jnp.where(lane == HEAD_DIM + n, piece, kept)
                g_ref[head, span, :] = kept.astype(bf16)

    step = k_ref.shape[1]
    lane_k = lax.broadcasted_iota(jnp.int32, (block, SLOT), 1)
    low_k = lane_k < HEAD_DIM
    for piece in range(step // block):
        span = pl.ds(piece * block, block)
        grads = []
        for head in range(2):
            keys, values = k_ref[head, span, :], v_ref[head, span, :]
            probs = jnp.exp(dot(keys, q_ref[head], NT))
            grad_scores = (probs * dot(values, g_ref[head], NT)).astype(bf16)
            grad_value = dot(probs.astype(bf16), g_ref[head])
            grad_key = dot(grad_scores, q_ref[head])
            acc_ref[head] += lax.dot_general(
                keys, grad_scores, (((0,), (0,)), ((), ())), preferred_element_type=f32
            )
            grads.append((grad_key, grad_value))
        grad_key, grad_value = (
            jnp.where(low_k, first, pltpu.roll(second, HEAD_DIM, 1))
            for first, second in zip(*grads)
        )
        place = pl.ds(pl.multiple_of(at * step + piece * block, block), block)
        grad_key = rope(grad_key, cos_ref[place, :], -sin_ref[place, :], lane_k)
        out_ref[place, SLOT : 2 * SLOT] = grad_key.astype(bf16)
        out_ref[place, 2 * SLOT :] = grad_value.astype(bf16)

    @pl.when(at == pl.num_programs(0) - 1)
    def _():
        grad_query = jnp.where(
            lax.broadcasted_iota(jnp.int32, (rows, SLOT), 1) < HEAD_DIM,
            acc_ref[0].T,
            pltpu.roll(acc_ref[1].T, HEAD_DIM, 1),
        )
        turned = rope(
            grad_query,
            cos_ref[...],
            -sin_ref[...],
            lax.broadcasted_iota(jnp.int32, (rows, SLOT), 1),
        )
        out_ref[:, :SLOT] = (turned * HEAD_DIM**-0.5).astype(bf16)


def attend_back(pair, query, keys, values, own, par, mixed, cosine, sine, block=256, step=512):
    heads, rows, _ = query.shape
    half = own.shape[0]
    full = pl.BlockSpec((2, rows, SLOT), lambda i: (pair, 0, 0))
    piece = pl.BlockSpec((2, step, SLOT), lambda i: (pair, i, 0))
    grad = pl.BlockSpec((half, SLOT), lambda i: (0, pair))
    return call(
        functools.partial(attend_back_kernel, block),
        "attend_back",
        (rows // step,),
        [
            full,
            piece,
            piece,
            grad,
            grad,
            pl.BlockSpec((rows, SLOT), lambda i: (0, pair)),
            whole((rows, SLOT)),
            whole((rows, SLOT)),
        ],
        whole((rows, 3 * SLOT)),
        shape((rows, 3 * SLOT), bf16),
        10 * 2 * rows * rows * SLOT,
        scratch=[pltpu.VMEM((2, rows, SLOT), bf16), pltpu.VMEM((2, SLOT, rows), f32)],
        exps=2 * rows * rows,
    )(query, keys, values, own, par, mixed, cosine, sine)


def normalize(value):
    mean = jnp.mean(value, axis=-1, keepdims=True)
    centred = value - mean
    inverse = lax.rsqrt(jnp.mean(centred * centred, axis=-1, keepdims=True) + EPS)
    return centred * inverse, inverse


def normalize_back(grad, xhat, inverse, gain):
    scaled = grad * gain
    return inverse * (
        scaled
        - jnp.mean(scaled, axis=-1, keepdims=True)
        - xhat * jnp.mean(scaled * xhat, axis=-1, keepdims=True)
    )


def fold_rows(value):
    return jnp.sum(value.reshape(-1, 8, value.shape[-1]), axis=0)


def attention_out_kernel(ctx_ref, got_ref, mine_ref, other_ref, tok_ref, gain_ref, xhat_ref, inv_ref, low_ref):
    branch = dot(ctx_ref[...], mine_ref[...], NT) + dot(got_ref[...], other_ref[...], NT)
    xhat, inverse = normalize(tok_ref[...].astype(f32) + branch)
    xhat_ref[...] = xhat
    inv_ref[...] = inverse
    low_ref[...] = (xhat * gain_ref[...]).astype(bf16)


def attention_out(ctx, got, mine, other, at, tokens, gain, block=256):
    rows, width = tokens.shape
    half = got.shape[1]
    piece = pl.BlockSpec((block, half), lambda i: (i, 0))
    row = pl.BlockSpec((block, width), lambda i: (i, 0))
    return call(
        attention_out_kernel,
        "attention_out",
        (rows // block,),
        [
            piece,
            piece,
            pl.BlockSpec((width, half), lambda i: (0, at // half)),
            whole(other.shape),
            row,
            whole((1, width)),
        ],
        [row, pl.BlockSpec((block, 1), lambda i: (i, 0)), row],
        [shape((rows, width), f32), shape((rows, 1), f32), shape((rows, width), bf16)],
        4 * rows * width * half,
    )(ctx, got, mine, other, tokens, gain)


def gate_up_kernel(block, x_ref, gate_ref, up_ref, act_ref, da_ref, db_ref):
    for piece in range(x_ref.shape[0] // block):
        span = pl.ds(piece * block, block)
        gate = dot(x_ref[span, :], gate_ref[...])
        up = dot(x_ref[span, :], up_ref[...])
        sigma = jax.nn.sigmoid(gate)
        swish = gate * sigma
        act_ref[span, :] = (swish * up).astype(bf16)
        da_ref[span, :] = (up * (sigma * (1.0 + gate * (1.0 - sigma)))).astype(bf16)
        db_ref[span, :] = swish.astype(bf16)


def gate_up(x, weights, units, tile=256, block=256):
    rows, width = x.shape
    count = units // tile
    out = pl.BlockSpec((rows, tile), lambda n: (0, n))
    return call(
        functools.partial(gate_up_kernel, block),
        "gate_up",
        (count,),
        [
            whole((rows, width)),
            pl.BlockSpec((width, tile), lambda n: (0, n)),
            pl.BlockSpec((width, tile), lambda n: (0, count + n)),
        ],
        [out] * 3,
        [shape((rows, units), bf16)] * 3,
        4 * rows * width * units,
    )(x, weights, weights)


def down_kernel(act_ref, down_ref, out_ref):
    out_ref[...] = dot(act_ref[...], down_ref[...], NT).astype(bf16)


def down(act, weights, at, block=256):
    rows, units = act.shape
    width = weights.shape[0]
    return call(
        down_kernel,
        "down",
        (rows // block,),
        [
            pl.BlockSpec((block, units), lambda i: (i, 0)),
            pl.BlockSpec((width, units), lambda i: (0, at // units)),
        ],
        pl.BlockSpec((block, width), lambda i: (i, 0)),
        shape((rows, width), bf16),
        2 * rows * width * units,
    )(act, weights)


def down_norm_kernel(
    act_ref, down_ref, got_ref, xhat_ref, cot_ref, gain_a_ref, gain_f_ref, out_ref, mid_ref, low_ref, sum_ref
):
    branch = dot(act_ref[...], down_ref[...], NT) + got_ref[...].astype(f32)
    xhat, inverse = normalize(xhat_ref[...] * gain_a_ref[...] + branch)
    gain = gain_f_ref[...]
    out_ref[...] = (xhat * gain).astype(bf16)
    grad = cot_ref[...].astype(f32)
    middle = normalize_back(grad, xhat, inverse, gain)
    mid_ref[...] = middle
    low_ref[...] = middle.astype(bf16)

    @pl.when(pl.program_id(0) == 0)
    def _():
        sum_ref[...] = jnp.zeros_like(sum_ref)

    sum_ref[...] += fold_rows(grad * xhat)


def down_norm(act, weights, at, got, xhat, cotangent, gain_a, gain_f, block=256):
    rows, units = act.shape
    width = weights.shape[0]
    row = pl.BlockSpec((block, width), lambda i: (i, 0))
    return call(
        down_norm_kernel,
        "down_norm",
        (rows // block,),
        [
            pl.BlockSpec((block, units), lambda i: (i, 0)),
            pl.BlockSpec((width, units), lambda i: (0, at // units)),
            row,
            row,
            row,
            whole((1, width)),
            whole((1, width)),
        ],
        [row, row, row, whole((8, width))],
        [
            shape((rows, width), bf16),
            shape((rows, width), f32),
            shape((rows, width), bf16),
            shape((8, width), f32),
        ],
        2 * rows * width * units,
    )(act, weights, got, xhat, cotangent, gain_a, gain_f)


def gate_up_back_kernel(block, g_ref, down_ref, da_ref, db_ref, gate_ref, up_ref):
    for piece in range(g_ref.shape[0] // block):
        span = pl.ds(piece * block, block)
        grad = dot(g_ref[span, :], down_ref[...])
        gate_ref[span, :] = (grad * da_ref[span, :].astype(f32)).astype(bf16)
        up_ref[span, :] = (grad * db_ref[span, :].astype(f32)).astype(bf16)


def gate_up_back(grad, weights, at, da, db, tile=256, block=256):
    rows, width = grad.shape
    units = da.shape[1]
    out = pl.BlockSpec((rows, tile), lambda n: (0, n))
    return call(
        functools.partial(gate_up_back_kernel, block),
        "gate_up_back",
        (units // tile,),
        [
            whole((rows, width)),
            pl.BlockSpec((width, tile), lambda n: (0, at // tile + n)),
            out,
            out,
        ],
        [out, out],
        [shape((rows, units), bf16)] * 2,
        2 * rows * width * units,
    )(grad, weights, da, db)


def hidden_back_kernel(gate_ref, up_ref, wg_ref, wu_ref, out_ref):
    out_ref[...] = (
        dot(gate_ref[...], wg_ref[...], NT) + dot(up_ref[...], wu_ref[...], NT)
    ).astype(bf16)


def hidden_back(gate, up, weights, block=256):
    rows, units = gate.shape
    width = weights.shape[0]
    piece = pl.BlockSpec((block, units), lambda i: (i, 0))
    return call(
        hidden_back_kernel,
        "hidden_back",
        (rows // block,),
        [
            piece,
            piece,
            pl.BlockSpec((width, units), lambda i: (0, 0)),
            pl.BlockSpec((width, units), lambda i: (0, 1)),
        ],
        pl.BlockSpec((block, width), lambda i: (i, 0)),
        shape((rows, width), bf16),
        4 * rows * width * units,
    )(gate, up, weights, weights)


def hidden_norm_back_kernel(
    gate_ref,
    up_ref,
    wg_ref,
    wu_ref,
    got_ref,
    mid_ref,
    xhat_ref,
    inv_ref,
    gain_ref,
    mine_ref,
    other_ref,
    res_ref,
    low_ref,
    keep_ref,
    send_ref,
    sum_ref,
):
    grad = (
        mid_ref[...]
        + got_ref[...].astype(f32)
        + dot(gate_ref[...], wg_ref[...], NT)
        + dot(up_ref[...], wu_ref[...], NT)
    )
    xhat = xhat_ref[...]
    residual = normalize_back(grad, xhat, inv_ref[...], gain_ref[...])
    res_ref[...] = residual
    low = residual.astype(bf16)
    low_ref[...] = low
    keep_ref[...] = dot(low, mine_ref[...]).astype(bf16)
    send_ref[...] = dot(low, other_ref[...]).astype(bf16)

    @pl.when(pl.program_id(0) == 0)
    def _():
        sum_ref[...] = jnp.zeros_like(sum_ref)

    sum_ref[...] += fold_rows(grad * xhat)


def hidden_norm_back(gate, up, weights, got, middle, xhat, inverse, gain, at, other, block=256):
    rows, units = gate.shape
    width, half = other.shape
    piece = pl.BlockSpec((block, units), lambda i: (i, 0))
    row = pl.BlockSpec((block, width), lambda i: (i, 0))
    part = pl.BlockSpec((block, half), lambda i: (i, 0))
    return call(
        hidden_norm_back_kernel,
        "hidden_norm_back",
        (rows // block,),
        [
            piece,
            piece,
            pl.BlockSpec((width, units), lambda i: (0, 0)),
            pl.BlockSpec((width, units), lambda i: (0, 1)),
            row,
            row,
            row,
            pl.BlockSpec((block, 1), lambda i: (i, 0)),
            whole((1, width)),
            pl.BlockSpec((width, half), lambda i: (0, at // half)),
            whole(other.shape),
        ],
        [row, row, part, part, whole((8, width))],
        [
            shape((rows, width), f32),
            shape((rows, width), bf16),
            shape((rows, half), bf16),
            shape((rows, half), bf16),
            shape((8, width), f32),
        ],
        4 * rows * width * (units + half),
    )(gate, up, weights, weights, got, middle, xhat, inverse, gain, weights, other)


def weight_grad_kernel(outer, inner, own_ref, par_ref, yo_ref, yp_ref, *refs):
    out_ref, turned_ref = refs[-2:]
    rows, width = own_ref.shape

    @pl.when(pl.program_id(0) == 0)
    def _():
        turned_ref[:, :rows] = own_ref[...].T
        turned_ref[:, rows:] = par_ref[...].T

    total = dot(turned_ref[:, :rows], yo_ref[...]) + dot(turned_ref[:, rows:], yp_ref[...])
    total = total.astype(bf16)
    if outer is None:
        out_ref[...] = total
    else:
        depth = width // (outer * inner)
        for hi in range(outer):
            for lo in range(inner):
                start = (hi * inner + lo) * depth
                out_ref[lo, hi] = total[start : start + depth]


def weight_grad(split, own, par, grad_own, grad_par, halves, columns, at, tile, into=None):
    rows, width = own.shape
    n = grad_own.shape[1]
    first = at // tile
    outer, inner = split if split else (None, None)
    if split:
        dims = (inner, outer, width // (outer * inner), columns)
        out = pl.BlockSpec((*dims[:3], tile), lambda i: (0, 0, 0, first + i))
    else:
        dims = (width, columns)
        out = pl.BlockSpec((width, tile), lambda i: (0, first + i))
    lower = halves
    operands = [own, par, grad_own, grad_par]
    specs = [
        whole((rows, width)),
        whole((rows, width)),
        pl.BlockSpec((rows, tile), lambda i: (0, i)),
        pl.BlockSpec((rows, tile), lambda i: (lower, i)),
    ]
    aliases = None
    if into is not None:
        operands.append(into)
        specs.append(pl.BlockSpec(memory_space=pl.ANY))
        aliases = {4: 0}
    return call(
        functools.partial(weight_grad_kernel, outer, inner),
        "weight_grad",
        (n // tile,),
        specs,
        out,
        shape(dims, bf16),
        4 * rows * width * n,
        scratch=[pltpu.VMEM((width, 2 * rows), bf16)],
        aliases=aliases,
    )(*operands)


def input_back_kernel(*refs):
    *piece_refs, w_ref, out_ref = refs
    joined = jnp.concatenate([ref[...] for ref in piece_refs], axis=1)
    out_ref[...] = dot(joined, w_ref[...], NT).astype(bf16)


def input_back_add_kernel(*refs):
    *piece_refs, w_ref, res_ref, got_ref, out_ref = refs
    joined = jnp.concatenate([ref[...] for ref in piece_refs], axis=1)
    total = dot(joined, w_ref[...], NT) + res_ref[...] + got_ref[...].astype(f32)
    out_ref[...] = total.astype(bf16)


def input_back(pieces, weights, lower, extra=(), block=256):
    rows = pieces[0].shape[0] // 2
    width, columns = weights.shape
    count = rows // block
    first = count if lower else 0
    row = pl.BlockSpec((block, width), lambda i: (i, 0))
    return call(
        input_back_add_kernel if extra else input_back_kernel,
        "input_back",
        (count,),
        [pl.BlockSpec((block, p.shape[1]), lambda i: (first + i, 0)) for p in pieces]
        + [whole(weights.shape)]
        + [row] * len(extra),
        row,
        shape((rows, width), bf16),
        2 * rows * width * columns,
    )(*pieces, weights, *extra)


def swap(value):
    return lax.ppermute(value, "mp", [(0, 1), (1, 0)])


def sum_everywhere(value, axes):
    for axis, size in axes:
        if size & (size - 1):
            return lax.psum(value, tuple(name for name, _ in axes))
    for axis, size in axes:
        step = 1
        while step < size:
            value = value + lax.ppermute(value, axis, [(i, i ^ step) for i in range(size)])
            step *= 2
    return value


def gather_rows(shard, split):
    if not split:
        return lax.all_gather(shard, ("hi", "lo"), axis=0, tiled=True)
    return lax.all_gather(shard, ("hi", "lo"), axis=0, tiled=True)


def scatter_rows(partial, split):
    if not split:
        return lax.psum_scatter(partial, ("hi", "lo"), scatter_dimension=0, tiled=True)
    once = lax.psum_scatter(partial, "lo", scatter_dimension=0, tiled=False)
    return lax.psum_scatter(once, "hi", scatter_dimension=0, tiled=False)


def row_tables(block_seq, block_len, core):
    blocks = SEQ_MAX // QLEN
    sequence, lengths = block_seq.reshape(blocks), block_len.reshape(blocks)
    index = jnp.arange(blocks, dtype=jnp.int32)
    same = sequence[:, None] == sequence[None, :]
    first = jnp.min(jnp.where(same, index[None, :], blocks), axis=1)
    table = jnp.stack([sequence, lengths, QLEN * (index - first)])
    turned = jnp.concatenate([table[:, blocks // 2 :], table[:, : blocks // 2]], axis=1)
    table = jnp.where(core == 0, table, turned)
    sequence, lengths, start = (jnp.repeat(part, QLEN)[:, None] for part in table)
    inside = (jnp.arange(SEQ_MAX, dtype=jnp.int32) % QLEN)[:, None]
    position = (start + inside).astype(f32)
    valid = inside < lengths

    lane = jnp.arange(SLOT, dtype=jnp.int32)
    half = HEAD_DIM // 2
    inverse = jnp.exp((lane % half).astype(f32) * (-2.0 * math.log(ROPE_BASE) / HEAD_DIM))
    angle = position * inverse[None, :]
    cosine = jnp.cos(angle)
    sine = jnp.sin(angle) * jnp.where(lane % HEAD_DIM < half, -1.0, 1.0)[None, :]

    column = (lane - HEAD_DIM)[None, :]
    in_mask = (column >= 0) & (column < blocks)
    match = column == sequence
    ext_q = jnp.where(in_mask & match, 1.0, 0.0).astype(bf16)
    ext_k = jnp.where(
        in_mask,
        jnp.where(match & valid, 0.0, MASKED),
        jnp.where((column >= 32) & (column < 35), -1.0, 0.0),
    ).astype(bf16)
    return cosine, sine, ext_q, ext_k


def local(
    split,
    axes,
    tokens,
    w_query,
    w_key,
    w_value,
    w_out,
    w_gate,
    w_up,
    w_down,
    attention_norm_gain,
    feedforward_norm_gain,
    block_seq,
    block_len,
    cotangent,
):
    depth, units = w_gate.shape
    mine = w_query.shape[1]
    pairs = mine // SLOT
    gain_a, gain_f = attention_norm_gain[None, :], feedforward_norm_gain[None, :]

    tokens_par = swap(tokens)
    qkv_shard = jnp.concatenate(
        [
            w[:, p * SLOT : (p + 1) * SLOT]
            for p in range(pairs)
            for w in (w_query, w_key, w_value)
        ],
        axis=1,
    )
    w_qkv = gather_rows(qkv_shard, split)
    at_up, at_down, at_out = units, 2 * units, 3 * units
    columns = at_out + mine
    w_rest = gather_rows(jnp.concatenate([w_gate, w_up, w_down.T, w_out.T], axis=1), split)
    cosine, sine, ext_q, ext_k = row_tables(block_seq, block_len, lax.axis_index("mp"))

    query, keys, values = project_qkv(tokens, tokens_par, w_qkv, cosine, sine, ext_q, ext_k)
    context, mixed, query = attend(query, keys, values)
    rows = tokens.shape[0]
    context_got = swap(context[rows:])
    out_other = swap(w_rest[:, at_out:])
    xhat_a, inverse_a, hidden = attention_out(
        context, context_got, w_rest, out_other, at_out, tokens, gain_a
    )
    hidden_par = swap(hidden)
    act, da, db = gate_up(hidden, w_rest, units)
    act_par, da_par, db_par = gate_up(hidden_par, w_rest, units)
    branch_got = swap(down(act_par, w_rest, at_down))
    output, middle, grad_branch, sum_f = down_norm(
        act, w_rest, at_down, branch_got, xhat_a, cotangent, gain_a, gain_f
    )

    grad_branch_par = swap(grad_branch)
    grad_gate, grad_up = gate_up_back(grad_branch, w_rest, at_down, da, db)
    grad_gate_par, grad_up_par = gate_up_back(grad_branch_par, w_rest, at_down, da_par, db_par)
    hidden_got = swap(hidden_back(grad_gate_par, grad_up_par, w_rest))
    tile = 512 if units % 512 == 0 else 128
    grads = weight_grad(
        split, grad_branch, grad_branch_par, act, act_par, 0, columns, at_down, tile
    )
    residual, grad_attn, grad_context, grad_context_send, sum_a = hidden_norm_back(
        grad_gate, grad_up, w_rest, hidden_got, middle, xhat_a, inverse_a, gain_a, at_out, out_other
    )
    grad_context_par = swap(grad_context_send)
    grad_attn_par = swap(grad_attn)
    grads = weight_grad(split, hidden, hidden_par, grad_gate, grad_gate_par, 0, columns, 0, tile, grads)
    grads = weight_grad(split, hidden, hidden_par, grad_up, grad_up_par, 0, columns, at_up, tile, grads)
    grads = weight_grad(
        split, grad_attn, grad_attn_par, context, context, 1, columns, at_out, mine, grads
    )
    grad_rest = scatter_rows(grads, split)
    gains = sum_everywhere(
        jnp.stack([jnp.sum(sum_a, axis=0), jnp.sum(sum_f, axis=0)]), axes
    )
    pieces = [
        attend_back(
            p, query, keys, values, grad_context, grad_context_par, mixed, cosine, sine
        )
        for p in range(pairs)
    ]
    input_got = swap(input_back(pieces, w_qkv, True))
    grads = None
    for p, piece in enumerate(pieces):
        grads = weight_grad(
            split, tokens, tokens_par, piece, piece, 1, 3 * mine, p * 3 * SLOT, 3 * SLOT, grads
        )
    grad_qkv = scatter_rows(grads, split)
    input_grad = input_back(pieces, w_qkv, False, (residual, input_got))

    grad_rest = grad_rest.astype(f32)
    grad_qkv = grad_qkv.astype(f32).reshape(depth, pairs, 3, SLOT)
    grad_query, grad_key, grad_value = (
        grad_qkv[:, :, n].reshape(depth, mine) for n in range(3)
    )
    return (
        output,
        input_grad,
        grad_query,
        grad_key,
        grad_value,
        grad_rest[:, at_out:].T,
        grad_rest[:, :at_up],
        grad_rest[:, at_up:at_down],
        grad_rest[:, at_down:at_out].T,
        gains[0],
        gains[1],
    )


def solution(mesh):
    n_dp, n_mp = mesh.shape["dp"], mesh.shape["mp"]
    inner = 4 if n_dp % 4 == 0 else 1
    outer = n_dp // inner
    fine = Mesh(mesh.devices.reshape(outer, inner, n_mp), ("hi", "lo", "mp"))
    dp = ("hi", "lo")
    rows = P(("hi", "lo", "mp"), None)
    axes = (("mp", n_mp), ("lo", inner), ("hi", outer))

    def layer(*operands):
        width = operands[0].shape[1]
        depth = width // n_dp
        split = (outer, inner) if depth % 16 == 0 and inner > 1 else None
        return jax.shard_map(
            functools.partial(local, split, axes),
            mesh=fine,
            in_specs=(
                rows,
                P(dp, "mp"),
                P(dp, "mp"),
                P(dp, "mp"),
                P("mp", dp),
                P(dp, "mp"),
                P(dp, "mp"),
                P("mp", dp),
                P(),
                P(),
                P(dp, None),
                P(dp, None),
                rows,
            ),
            out_specs=(
                rows,
                rows,
                P(dp, "mp"),
                P(dp, "mp"),
                P(dp, "mp"),
                P("mp", dp),
                P(dp, "mp"),
                P(dp, "mp"),
                P("mp", dp),
                P(),
                P(),
            ),
            check_vma=False,
        )(*operands)

    return layer
```

```python
import functools
import math

import jax
import jax.numpy as jnp
from jax import lax
from jax.experimental import pallas as pl
from jax.experimental.pallas import tpu as pltpu
from jax.sharding import Mesh
from jax.sharding import PartitionSpec as P

HEAD_DIM = 64
SEQ_MAX = 2048
QLEN = 64
EPS = 1e-05
ROPE_BASE = 1000.0
MASKED = -1e30
SLOT = 128

bf16 = jnp.bfloat16
f32 = jnp.float32

NN = (((1,), (0,)), ((), ()))
NT = (((1,), (1,)), ((), ()))


def dot(left, right, dims=NN):
    return lax.dot_general(left, right, dims, preferred_element_type=f32)


def call(kernel, name, grid, in_specs, out_specs, out_shape, flops, scratch=(), aliases=None, exps=0):
    def run(*operands):
        outs = out_shape if isinstance(out_shape, (list, tuple)) else [out_shape]
        moved = sum(math.prod(o.shape) * o.dtype.itemsize for o in (*operands, *outs))
        return pl.pallas_call(
            kernel,
            name=name,
            grid=grid,
            in_specs=in_specs,
            out_specs=out_specs,
            out_shape=out_shape,
            scratch_shapes=list(scratch),
            input_output_aliases=aliases or {},
            cost_estimate=pl.CostEstimate(
                flops=int(flops), bytes_accessed=int(moved), transcendentals=int(exps)
            ),
            compiler_params=pltpu.CompilerParams(vmem_limit_bytes=60 * 1024 * 1024),
        )(*operands)

    return run


def shape(dims, dtype):
    return jax.ShapeDtypeStruct(dims, dtype)


def whole(dims):
    return pl.BlockSpec(dims, lambda *_: (0,) * len(dims))


def rope(value, cosine, sine, lane):
    half = HEAD_DIM // 2
    lanes = value.shape[-1]
    swapped = jnp.where(
        lane % HEAD_DIM < half,
        pltpu.roll(value, lanes - half, 1),
        pltpu.roll(value, half, 1),
    )
    return value * cosine + swapped * sine


def qkv_kernel(own_blocks, places, me_ref, own_ref, par_ref, *refs):
    piece_refs = refs[: len(places)]
    cos_ref, sin_ref, eq_ref, ek_ref, q_ref, k_ref, v_ref, w_ref, turned_ref = refs[len(places) :]

    @pl.when(pl.program_id(0) == 0)
    def _():
        for piece_ref, (starts, column) in zip(piece_refs, places):
            _, depth, width = piece_ref.shape
            for n, start in enumerate(starts):
                row = pl.multiple_of((start ^ me_ref[0]) * depth, depth)
                w_ref[pl.ds(row, depth), column : column + width] = piece_ref[n]

    rows = jnp.where(pl.program_id(0) < own_blocks, own_ref[...], par_ref[...])
    turned_ref[...] = rows.T
    lane = lax.broadcasted_iota(jnp.int32, (rows.shape[0], SLOT), 1)
    low = lane < HEAD_DIM
    ones = jnp.where((lane >= HEAD_DIM) & (lane < HEAD_DIM + 3), -1.0, 0.0)
    cosine, sine = cos_ref[...], sin_ref[...]
    ext_q, ext_k = eq_ref[...].astype(f32), ek_ref[...].astype(f32)
    for pair in range(q_ref.shape[0] // 2):
        base = pair * 3 * SLOT
        mixed = dot(rows, w_ref[:, base : base + 3 * SLOT])
        query = rope(mixed[:, :SLOT], cosine, sine, lane) * HEAD_DIM**-0.5
        key = rope(mixed[:, SLOT : 2 * SLOT], cosine, sine, lane)
        value = mixed[:, 2 * SLOT :]
        for ref, data, ext in ((q_ref, query, ext_q), (k_ref, key, ext_k), (v_ref, value, ones)):
            ref[2 * pair] = jnp.where(low, data, ext).astype(bf16)
            ref[2 * pair + 1] = jnp.where(low, pltpu.roll(data, HEAD_DIM, 1), ext).astype(bf16)


def project_qkv(me, own, par, pieces, cosine, sine, ext_q, ext_k, block=512):
    rows, width = own.shape
    arrays = [piece[0] for piece in pieces]
    places = [piece[1:] for piece in pieces]
    columns = max(column + array.shape[2] for array, _, column in pieces)
    heads = columns // (3 * HEAD_DIM)
    count = rows // block
    table = pl.BlockSpec((block, SLOT), lambda i: (i, 0))
    out = pl.BlockSpec((heads, block, SLOT), lambda i: (0, i, 0))
    return call(
        functools.partial(qkv_kernel, count, places),
        "project_qkv",
        (2 * count,),
        [
            pl.BlockSpec(memory_space=pltpu.SMEM),
            pl.BlockSpec((block, width), lambda i: (jnp.minimum(i, count - 1), 0)),
            pl.BlockSpec((block, width), lambda i: (jnp.maximum(i - count, 0), 0)),
            *(whole(array.shape) for array in arrays),
            table,
            table,
            table,
            table,
        ],
        [out] * 3 + [whole((width, columns)), pl.BlockSpec((width, block), lambda i: (0, i))],
        [shape((heads, 2 * rows, SLOT), bf16)] * 3
        + [shape((width, columns), bf16), shape((width, 2 * rows), bf16)],
        4 * rows * width * columns,
    )(me, own, par, *arrays, cosine, sine, ext_q, ext_k)


def split_three(value):
    first = value.astype(bf16).astype(f32)
    second = (value - first).astype(bf16).astype(f32)
    return first, second, value - first - second


def attend_kernel(block, q_ref, k_ref, v_ref, ctx_ref, mix_ref, q2_ref):
    lane = lax.broadcasted_iota(jnp.int32, (block, SLOT), 1)
    low = lane < HEAD_DIM
    for piece in range(q_ref.shape[1] // block):
        rows = pl.ds(piece * block, block)
        mixed = []
        for head in range(2):
            query = q_ref[head, rows, :]
            scores = dot(query, k_ref[head], NT)
            peak = jnp.max(scores, axis=-1, keepdims=True)
            expo = jnp.exp(scores - peak).astype(bf16)
            total_mix = dot(expo, v_ref[head])
            total = -total_mix[:, HEAD_DIM : HEAD_DIM + 1]
            mixed.append(total_mix * (1.0 / total))
            parts = split_three(peak + jnp.log(total))
            kept = query.astype(f32)
            for at, part in enumerate(parts):
                kept = jnp.where(lane == HEAD_DIM + 32 + at, part, kept)
            q2_ref[head, rows, :] = kept.astype(bf16)
        both = jnp.where(low, mixed[0], pltpu.roll(mixed[1], HEAD_DIM, 1))
        mix_ref[rows, :] = both
        ctx_ref[rows, :] = both.astype(bf16)


def attend(query, keys, values, block=512, step=1024):
    heads, rows, _ = query.shape
    piece = pl.BlockSpec((2, step, SLOT), lambda p, i: (p, i, 0))
    full = pl.BlockSpec((2, rows, SLOT), lambda p, i: (p, 0, 0))
    out = pl.BlockSpec((step, SLOT), lambda p, i: (i, p))
    width = heads * HEAD_DIM
    return call(
        functools.partial(attend_kernel, block),
        "attend",
        (heads // 2, rows // step),
        [piece, full, full],
        [out, out, piece],
        [shape((rows, width), bf16), shape((rows, width), f32), shape(query.shape, bf16)],
        4 * heads * rows * rows * SLOT,
        exps=heads * rows * rows,
    )(query, keys, values)


def attend_back_kernel(
    block, q_ref, k_ref, v_ref, own_ref, par_ref, mix_ref, cos_ref, sin_ref, out_ref, g_ref, acc_ref
):
    at = pl.program_id(0)
    rows = q_ref.shape[1]
    half = own_ref.shape[0]
    lane = lax.broadcasted_iota(jnp.int32, (half, SLOT), 1)
    low = lane < HEAD_DIM

    @pl.when(at == 0)
    def _():
        acc_ref[...] = jnp.zeros_like(acc_ref)
        for part, grad_ref in enumerate((own_ref, par_ref)):
            span = pl.ds(part * half, half)
            grad = grad_ref[...].astype(f32)
            product = grad * mix_ref[span, :]
            for head in range(2):
                mine = low if head == 0 else ~low
                delta = jnp.sum(jnp.where(mine, product, 0.0), axis=-1, keepdims=True)
                kept = grad if head == 0 else pltpu.roll(grad, HEAD_DIM, 1)
                kept = jnp.where(low, kept, 0.0)
                for n, piece in enumerate(split_three(delta)):
                    kept = jnp.where(lane == HEAD_DIM + n, piece, kept)
                g_ref[head, span, :] = kept.astype(bf16)

    step = k_ref.shape[1]
    lane_k = lax.broadcasted_iota(jnp.int32, (block, SLOT), 1)
    low_k = lane_k < HEAD_DIM
    for piece in range(step // block):
        span = pl.ds(piece * block, block)
        grads = []
        for head in range(2):
            keys, values = k_ref[head, span, :], v_ref[head, span, :]
            probs = jnp.exp(dot(keys, q_ref[head], NT))
            grad_scores = (probs * dot(values, g_ref[head], NT)).astype(bf16)
            grad_value = dot(probs.astype(bf16), g_ref[head])
            grad_key = dot(grad_scores, q_ref[head])
            acc_ref[head] += lax.dot_general(
                keys, grad_scores, (((0,), (0,)), ((), ())), preferred_element_type=f32
            )
            grads.append((grad_key, grad_value))
        grad_key, grad_value = (
            jnp.where(low_k, first, pltpu.roll(second, HEAD_DIM, 1))
            for first, second in zip(*grads)
        )
        place = pl.ds(pl.multiple_of(at * step + piece * block, block), block)
        grad_key = rope(grad_key, cos_ref[place, :], -sin_ref[place, :], lane_k)
        out_ref[place, SLOT : 2 * SLOT] = grad_key.astype(bf16)
        out_ref[place, 2 * SLOT :] = grad_value.astype(bf16)

    @pl.when(at == pl.num_programs(0) - 1)
    def _():
        grad_query = jnp.where(
            lax.broadcasted_iota(jnp.int32, (rows, SLOT), 1) < HEAD_DIM,
            acc_ref[0].T,
            pltpu.roll(acc_ref[1].T, HEAD_DIM, 1),
        )
        turned = rope(
            grad_query,
            cos_ref[...],
            -sin_ref[...],
            lax.broadcasted_iota(jnp.int32, (rows, SLOT), 1),
        )
        out_ref[:, :SLOT] = (turned * HEAD_DIM**-0.5).astype(bf16)


def attend_back(pair, query, keys, values, own, par, mixed, cosine, sine, block=512, step=512):
    heads, rows, _ = query.shape
    half = own.shape[0]
    full = pl.BlockSpec((2, rows, SLOT), lambda i: (pair, 0, 0))
    piece = pl.BlockSpec((2, step, SLOT), lambda i: (pair, i, 0))
    grad = pl.BlockSpec((half, SLOT), lambda i: (0, pair))
    return call(
        functools.partial(attend_back_kernel, block),
        "attend_back",
        (rows // step,),
        [
            full,
            piece,
            piece,
            grad,
            grad,
            pl.BlockSpec((rows, SLOT), lambda i: (0, pair)),
            whole((rows, SLOT)),
            whole((rows, SLOT)),
        ],
        whole((rows, 3 * SLOT)),
        shape((rows, 3 * SLOT), bf16),
        10 * 2 * rows * rows * SLOT,
        scratch=[pltpu.VMEM((2, rows, SLOT), bf16), pltpu.VMEM((2, SLOT, rows), f32)],
        exps=2 * rows * rows,
    )(query, keys, values, own, par, mixed, cosine, sine)


def normalize(value):
    mean = jnp.mean(value, axis=-1, keepdims=True)
    centred = value - mean
    inverse = lax.rsqrt(jnp.mean(centred * centred, axis=-1, keepdims=True) + EPS)
    return centred * inverse, inverse


def normalize_back(grad, xhat, inverse, gain):
    scaled = grad * gain
    return inverse * (
        scaled
        - jnp.mean(scaled, axis=-1, keepdims=True)
        - xhat * jnp.mean(scaled * xhat, axis=-1, keepdims=True)
    )


def fold_rows(value):
    return jnp.sum(value.reshape(-1, 8, value.shape[-1]), axis=0)


def attention_out_kernel(
    ctx_ref, got_ref, mine_ref, other_ref, tok_ref, gain_ref, xhat_ref, inv_ref, low_ref, turned_ref
):
    branch = dot(ctx_ref[...], mine_ref[...], NT) + dot(got_ref[...], other_ref[...], NT)
    xhat, inverse = normalize(tok_ref[...].astype(f32) + branch)
    xhat_ref[...] = xhat
    inv_ref[...] = inverse
    low = (xhat * gain_ref[...]).astype(bf16)
    low_ref[...] = low
    turned_ref[...] = low.T


def attention_out(ctx, got, mine, other, at, tokens, gain, block=256):
    rows, width = tokens.shape
    half = got.shape[1]
    piece = pl.BlockSpec((block, half), lambda i: (i, 0))
    row = pl.BlockSpec((block, width), lambda i: (i, 0))
    return call(
        attention_out_kernel,
        "attention_out",
        (rows // block,),
        [
            piece,
            piece,
            pl.BlockSpec((width, half), lambda i: (0, at // half)),
            whole(other.shape),
            row,
            whole((1, width)),
        ],
        [
            row,
            pl.BlockSpec((block, 1), lambda i: (i, 0)),
            row,
            pl.BlockSpec((width, block), lambda i: (0, i)),
        ],
        [
            shape((rows, width), f32),
            shape((rows, 1), f32),
            shape((rows, width), bf16),
            shape((width, rows), bf16),
        ],
        4 * rows * width * half,
    )(ctx, got, mine, other, tokens, gain)


def gate_up_tile(x_ref, gate_w, up_w, down_w, act_ref, da_ref, db_ref, acc_ref, block):
    for piece in range(x_ref.shape[0] // block):
        span = pl.ds(piece * block, block)
        gate = dot(x_ref[span, :], gate_w)
        up = dot(x_ref[span, :], up_w)
        sigma = jax.nn.sigmoid(gate)
        swish = gate * sigma
        act = (swish * up).astype(bf16)
        act_ref[span, :] = act
        da_ref[span, :] = (up * (sigma * (1.0 + gate * (1.0 - sigma)))).astype(bf16)
        db_ref[span, :] = swish.astype(bf16)
        acc_ref[span, :] += dot(act, down_w, NT)


def forward_first_kernel(block, x_ref, gate_ref, up_ref, down_ref, act_ref, da_ref, db_ref, acc_ref):
    @pl.when(pl.program_id(0) == 0)
    def _():
        acc_ref[...] = jnp.zeros_like(acc_ref)

    gate_up_tile(
        x_ref, gate_ref[...], up_ref[...], down_ref[...], act_ref, da_ref, db_ref, acc_ref, block
    )


def forward_first(x, weights, units, tile=512, block=1024):
    rows, width = x.shape
    count = units // tile
    out = pl.BlockSpec((rows, tile), lambda n: (0, n))
    return call(
        functools.partial(forward_first_kernel, block),
        "forward_first",
        (count,),
        [whole((rows, width))]
        + [pl.BlockSpec((width, tile), lambda n, at=at: (0, at * count + n)) for at in range(3)],
        [out] * 3 + [whole((rows, width))],
        [shape((rows, units), bf16)] * 3 + [shape((rows, width), f32)],
        6 * rows * width * units,
    )(x, weights, weights, weights)


def turn_kernel(
    block,
    count,
    x_ref,
    gate_w_ref,
    up_w_ref,
    down_w_ref,
    part_ref,
    xhat_ref,
    cot_ref,
    gain_a_ref,
    gain_f_ref,
    xt_ref,
    out_ref,
    mid_ref,
    low_ref,
    turned_ref,
    sum_ref,
    grads_ref,
    act_ref,
    da_ref,
    db_ref,
    gate_ref,
    up_ref,
    acc_ref,
):
    at = pl.program_id(0)

    @pl.when(at == 0)
    def _():
        acc_ref[...] = part_ref[...]

    @pl.when(at < count)
    def _():
        gate_up_tile(
            x_ref,
            gate_w_ref[...],
            up_w_ref[...],
            down_w_ref[...],
            act_ref.at[at],
            da_ref.at[at],
            db_ref.at[at],
            acc_ref,
            block,
        )

    @pl.when(at == count - 1)
    def _():
        gain_a, gain_f = gain_a_ref[...], gain_f_ref[...]
        small = 256
        total = jnp.zeros_like(sum_ref)
        for piece in range(x_ref.shape[0] // small):
            span = pl.ds(piece * small, small)
            xhat, inverse = normalize(xhat_ref[span, :] * gain_a + acc_ref[span, :])
            out_ref[span, :] = (xhat * gain_f).astype(bf16)
            grad = cot_ref[span, :].astype(f32)
            middle = normalize_back(grad, xhat, inverse, gain_f)
            mid_ref[span, :] = middle
            low = middle.astype(bf16)
            low_ref[span, :] = low
            turned_ref[:, span] = low.T
            total += fold_rows(grad * xhat)
        sum_ref[...] = total

    @pl.when(at >= count)
    def _():
        tile = at - count
        small = 512
        for piece in range(x_ref.shape[0] // small):
            span = pl.ds(piece * small, small)
            grad = dot(low_ref[span, :], down_w_ref[...])
            gate = (grad * da_ref[tile, span, :].astype(f32)).astype(bf16)
            up = (grad * db_ref[tile, span, :].astype(f32)).astype(bf16)
            gate_ref[span, :] = gate
            up_ref[span, :] = up
            mid_ref[span, :] += dot(gate, gate_w_ref[...], NT) + dot(up, up_w_ref[...], NT)
        grads_ref[0] = dot(xt_ref[...], gate_ref[...]).astype(bf16)
        grads_ref[1] = dot(xt_ref[...], up_ref[...]).astype(bf16)
        grads_ref[2] = dot(turned_ref[...], act_ref[tile]).astype(bf16)


def forward_and_back(x, turned, weights, units, part, xhat, cotangent, gain_a, gain_f, tile=512, block=1024):
    rows, width = x.shape
    count = units // tile
    full, gain = whole((rows, width)), whole((1, width))
    flat = whole((width, rows))

    def weight(part):
        return pl.BlockSpec((width, tile), lambda n: (0, part * count + lax.rem(n, count)))

    return call(
        functools.partial(turn_kernel, block, count),
        "forward_and_back",
        (2 * count,),
        [full, weight(0), weight(1), weight(2), full, full, full, gain, gain, flat],
        [
            full,
            full,
            full,
            flat,
            whole((8, width)),
            pl.BlockSpec((3, width, tile), lambda n: (0, 0, jnp.maximum(n - count, 0))),
        ],
        [
            shape((rows, width), bf16),
            shape((rows, width), f32),
            shape((rows, width), bf16),
            shape((width, rows), bf16),
            shape((8, width), f32),
            shape((3, width, units), bf16),
        ],
        18 * rows * width * units,
        scratch=[pltpu.VMEM((count, rows, tile), bf16)] * 3
        + [pltpu.VMEM((rows, tile), bf16)] * 2
        + [pltpu.VMEM((rows, width), f32)],
    )(x, weights, weights, weights, part, xhat, cotangent, gain_a, gain_f, turned)


def backward_kernel(block, final, g_ref, gate_w_ref, up_w_ref, down_w_ref, da_ref, db_ref, part_ref, *refs):
    if final:
        xhat_ref, inv_ref, gain_ref, mine_ref, other_ref, *refs = refs
        gate_ref, up_ref, res_ref, turned_ref, keep_ref, send_ref, sum_ref, acc_ref = refs
    else:
        gate_ref, up_ref, acc_ref = refs

    @pl.when(pl.program_id(0) == 0)
    def _():
        acc_ref[...] = part_ref[...]

    for piece in range(g_ref.shape[0] // block):
        span = pl.ds(piece * block, block)
        grad = dot(g_ref[span, :], down_w_ref[...])
        gate = (grad * da_ref[span, :].astype(f32)).astype(bf16)
        up = (grad * db_ref[span, :].astype(f32)).astype(bf16)
        gate_ref[span, :] = gate
        up_ref[span, :] = up
        acc_ref[span, :] += dot(gate, gate_w_ref[...], NT) + dot(up, up_w_ref[...], NT)

    if not final:
        return

    @pl.when(pl.program_id(0) == pl.num_programs(0) - 1)
    def _():
        gain = gain_ref[...]
        small = 256
        total = jnp.zeros_like(sum_ref)
        for piece in range(g_ref.shape[0] // small):
            span = pl.ds(piece * small, small)
            grad, xhat = acc_ref[span, :], xhat_ref[span, :]
            residual = normalize_back(grad, xhat, inv_ref[span, :], gain)
            res_ref[span, :] = residual
            low = residual.astype(bf16)
            turned_ref[:, span] = low.T
            keep_ref[span, :] = dot(low, mine_ref[...]).astype(bf16)
            send_ref[span, :] = dot(low, other_ref[...]).astype(bf16)
            total += fold_rows(grad * xhat)
        sum_ref[...] = total


def backward(grad, weights, da, db, part, final=(), at=0, tile=512, block=512):
    rows, width = grad.shape
    units = da.shape[1]
    count = units // tile
    full = whole((rows, width))
    out = pl.BlockSpec((rows, tile), lambda n: (0, n))
    specs = [full]
    specs += [pl.BlockSpec((width, tile), lambda n, p=p: (0, p * count + n)) for p in range(3)]
    specs += [out, out, full]
    outs, shapes = [out, out], [shape((rows, units), bf16)] * 2
    flops = 6 * rows * width * units
    if final:
        half = final[-1].shape[1]
        part_out = whole((rows, half))
        specs += [
            full,
            whole((rows, 1)),
            whole((1, width)),
            pl.BlockSpec((width, half), lambda n: (0, at // half)),
            whole((width, half)),
        ]
        outs += [full, whole((width, rows)), part_out, part_out, whole((8, width))]
        shapes += [
            shape((rows, width), f32),
            shape((width, rows), bf16),
            shape((rows, half), bf16),
            shape((rows, half), bf16),
            shape((8, width), f32),
        ]
        flops += 4 * rows * width * half
        scratch = [pltpu.VMEM((rows, width), f32)]
    else:
        outs.append(full)
        shapes.append(shape((rows, width), f32))
        scratch = []
    return call(
        functools.partial(backward_kernel, block, bool(final)),
        "backward_last" if final else "backward_first",
        (count,),
        specs,
        outs,
        shapes,
        flops,
        scratch=scratch,
    )(grad, weights, weights, weights, da, db, part, *final)


def mirrored(index, count):
    bits = count.bit_length() - 1
    return sum(((index >> bit) & 1) << (bits - 1 - bit) for bit in range(bits))


def weight_grad_kernel(order, me_ref, own_ref, par_ref, yo_ref, yp_ref, *refs):
    out_ref = refs[-1]
    total = dot(own_ref[...], yo_ref[...]) + dot(par_ref[...], yp_ref[...])
    total = total.astype(bf16)
    if order is None:
        out_ref[...] = total
        return
    count = math.prod(order)
    depth = total.shape[0] // count
    for shard in range(count):
        place = mirrored(shard ^ me_ref[0], count)
        out_ref[place] = total[shard * depth : (shard + 1) * depth]


def weight_grad(order, me, own, par, grad, columns, at, into=None):
    rows, n = grad.shape[0] // 2, grad.shape[1]
    width = own[0].shape[0]
    first = at // n
    if order:
        count = math.prod(order)
        dims = (count, width // count, columns)
        out = pl.BlockSpec((*dims[:2], n), lambda i: (0, 0, first))
    else:
        dims = (width, columns)
        out = pl.BlockSpec((width, n), lambda i: (0, first))
    operands = [me, own[0], par[0], grad, grad]
    specs = [
        pl.BlockSpec(memory_space=pltpu.SMEM),
        pl.BlockSpec((width, rows), lambda i: (0, own[1])),
        pl.BlockSpec((width, rows), lambda i: (0, par[1])),
        pl.BlockSpec((rows, n), lambda i: (0, 0)),
        pl.BlockSpec((rows, n), lambda i: (1, 0)),
    ]
    aliases = None
    if into is not None:
        operands.append(into)
        specs.append(pl.BlockSpec(memory_space=pl.ANY))
        aliases = {5: 0}
    return call(
        functools.partial(weight_grad_kernel, order),
        "weight_grad",
        (1,),
        specs,
        out,
        shape(dims, bf16),
        4 * rows * width * n,
        aliases=aliases,
    )(*operands)


def dense_grad_kernel(outer, inner, tiles, add, hi_ref, *refs):
    segments = len(tiles)
    row_refs, grad_refs, refs = refs[:segments], refs[segments : 2 * segments], refs[2 * segments :]
    out_ref = refs[-1]
    at = pl.program_id(0)
    first = 0
    for row_ref, grad_ref, count in zip(row_refs, grad_refs, tiles):

        def write(row_ref=row_ref, grad_ref=grad_ref):
            total = dot(row_ref[...], grad_ref[...])
            if add:
                total = total + refs[0][0].astype(f32)
            total = total.astype(bf16)
            if outer is None:
                out_ref[...] = total
            else:
                depth = total.shape[0] // (outer * inner)
                for hi in range(outer):
                    place = mirrored(hi ^ hi_ref[0], outer)
                    for lo in range(inner):
                        start = (hi * inner + lo) * depth
                        out_ref[lo, place] = total[start : start + depth]

        pl.when((at >= first) & (at < first + count))(write)
        first += count


def dense_grad(me_hi, segments, tile, split=None, add=None):
    width, rows = segments[0][0].shape
    tiles = [columns // tile for *_, columns in segments]
    columns = sum(tiles) * tile
    starts = [sum(tiles[:n]) for n in range(len(tiles))]

    def spec(at, start, count):
        return pl.BlockSpec((rows, tile), lambda i: (0, at // tile + jnp.clip(i - start, 0, count - 1)))

    operands = [me_hi] + [x for x, *_ in segments] + [y for _, y, *_ in segments]
    specs = [pl.BlockSpec(memory_space=pltpu.SMEM)] + [whole((width, rows)) for _ in segments]
    specs += [spec(at, start, n) for (_, _, at, _), start, n in zip(segments, starts, tiles)]
    flat = pl.BlockSpec((width, tile), lambda i: (0, i))
    if add is not None:
        operands.append(add)
        per = add.shape[2] // tile
        specs.append(pl.BlockSpec((1, width, tile), lambda i: (i // per, 0, lax.rem(i, per))))
    outer, inner = split if split else (None, None)
    if split:
        dims = (inner, outer, width // (outer * inner), columns)
        out = pl.BlockSpec((*dims[:3], tile), lambda i: (0, 0, 0, i))
    else:
        dims, out = (width, columns), flat
    return call(
        functools.partial(dense_grad_kernel, outer, inner, tiles, add is not None),
        "dense_grad",
        (columns // tile,),
        specs,
        out,
        shape(dims, bf16),
        2 * rows * width * columns,
    )(*operands)


def input_back_kernel(*refs):
    *piece_refs, w_ref, out_ref = refs
    joined = jnp.concatenate([ref[...] for ref in piece_refs], axis=1)
    out_ref[...] = dot(joined, w_ref[...], NT).astype(bf16)


def input_back_add_kernel(*refs):
    *piece_refs, w_ref, res_ref, got_ref, out_ref = refs
    joined = jnp.concatenate([ref[...] for ref in piece_refs], axis=1)
    total = dot(joined, w_ref[...], NT) + res_ref[...] + got_ref[...].astype(f32)
    out_ref[...] = total.astype(bf16)


def input_back(pieces, weights, lower, extra=(), block=256):
    rows = pieces[0].shape[0] // 2
    width, columns = weights.shape
    count = rows // block
    first = count if lower else 0
    row = pl.BlockSpec((block, width), lambda i: (i, 0))
    return call(
        input_back_add_kernel if extra else input_back_kernel,
        "input_back",
        (count,),
        [pl.BlockSpec((block, p.shape[1]), lambda i: (first + i, 0)) for p in pieces]
        + [whole(weights.shape)]
        + [row] * len(extra),
        row,
        shape((rows, width), bf16),
        2 * rows * width * columns,
    )(*pieces, weights, *extra)


def swap(value):
    return lax.ppermute(value, "mp", [(0, 1), (1, 0)])


def sum_everywhere(value, axes):
    for axis, size in axes:
        if size & (size - 1):
            return lax.psum(value, tuple(name for name, _ in axes))
    for axis, size in axes:
        step = 1
        while step < size:
            value = value + lax.ppermute(value, axis, [(i, i ^ step) for i in range(size)])
            step *= 2
    return value


def exchange(value, axis, size, step):
    return lax.ppermute(value, axis, [(i, i ^ step) for i in range(size)])


def gather_rows(shard):
    return lax.all_gather(shard, ("hi", "lo"), axis=0, tiled=True)


def gather_pieces(shard, split):
    outer, inner = split
    held = shard[None]
    step = outer // 2
    starts = [0]
    while step:
        held = jnp.concatenate([held, exchange(held, "hi", outer, step)])
        starts = starts + [start ^ (step * inner) for start in starts]
        step //= 2
    cut = shard.shape[1] // (2 * SLOT) * SLOT
    pieces = [(held, starts, 0)]
    for column, width, bits in ((0, cut, (1, 2)), (cut, shard.shape[1] - cut, (2, 1))):
        part = lax.slice_in_dim(held, column, column + width, axis=2)
        once = exchange(part, "lo", inner, bits[0])
        twice = exchange(jnp.concatenate([part, once]), "lo", inner, bits[1])
        beside = [start ^ bits[0] for start in starts]
        pieces.append((once, beside, column))
        pieces.append((twice, [start ^ bits[1] for start in starts + beside], column))
    return pieces


def scatter_first(partial, split):
    if not split:
        return lax.psum_scatter(partial, ("hi", "lo"), scatter_dimension=0, tiled=True)
    return lax.psum_scatter(partial, "lo", scatter_dimension=0, tiled=False)


def to_terms(value, columns):
    terms = jnp.stack([term.astype(bf16) for term in split_three(value)])
    whole_rows = 16 * columns
    flat = terms.reshape(-1)
    return jnp.pad(flat, (0, -flat.size % whole_rows)).reshape(-1, columns)


def from_terms(rows, dims):
    count = 3 * math.prod(dims)
    return jnp.sum(rows.reshape(-1)[:count].reshape(3, *dims).astype(f32), axis=0)


def send_half(partial, axis, size, step, rider=None):
    half, (depth, columns) = partial.shape[0] // 2, partial.shape[1:]
    message = partial[half:].reshape(half * depth, columns)
    terms = None
    if rider is not None:
        terms = to_terms(rider, columns)
        message = jnp.concatenate([message, terms])
        rider = from_terms(terms, rider.shape)
    return exchange(message, axis, size, step), (partial[:half], rider)


def take_half(got, held):
    kept, rider = held
    rows = kept.shape[0] * kept.shape[1]
    if rider is not None:
        rider = rider + from_terms(got[rows:], rider.shape)
        got = got[:rows]
    return (kept.astype(f32) + got.reshape(kept.shape).astype(f32)).astype(bf16), rider


def tie(*values):
    return lax.optimization_barrier(values)


def row_tables(block_seq, block_len, core):
    blocks = SEQ_MAX // QLEN
    sequence, lengths = block_seq.reshape(blocks), block_len.reshape(blocks)
    index = jnp.arange(blocks, dtype=jnp.int32)
    same = sequence[:, None] == sequence[None, :]
    first = jnp.min(jnp.where(same, index[None, :], blocks), axis=1)
    table = jnp.stack([sequence, lengths, QLEN * (index - first)])
    turned = jnp.concatenate([table[:, blocks // 2 :], table[:, : blocks // 2]], axis=1)
    table = jnp.where(core == 0, table, turned)
    sequence, lengths, start = (jnp.repeat(part, QLEN)[:, None] for part in table)
    inside = (jnp.arange(SEQ_MAX, dtype=jnp.int32) % QLEN)[:, None]
    position = (start + inside).astype(f32)
    valid = inside < lengths

    lane = jnp.arange(SLOT, dtype=jnp.int32)
    half = HEAD_DIM // 2
    inverse = jnp.exp((lane % half).astype(f32) * (-2.0 * math.log(ROPE_BASE) / HEAD_DIM))
    angle = position * inverse[None, :]
    cosine = jnp.cos(angle)
    sine = jnp.sin(angle) * jnp.where(lane % HEAD_DIM < half, -1.0, 1.0)[None, :]

    column = (lane - HEAD_DIM)[None, :]
    in_mask = (column >= 0) & (column < blocks)
    match = column == sequence
    ext_q = jnp.where(in_mask & match, 1.0, 0.0).astype(bf16)
    ext_k = jnp.where(
        in_mask,
        jnp.where(match & valid, 0.0, MASKED),
        jnp.where((column >= 32) & (column < 35), -1.0, 0.0),
    ).astype(bf16)
    return cosine, sine, ext_q, ext_k


def local(
    split,
    axes,
    tokens,
    w_query,
    w_key,
    w_value,
    w_out,
    w_gate,
    w_up,
    w_down,
    attention_norm_gain,
    feedforward_norm_gain,
    block_seq,
    block_len,
    cotangent,
):
    depth, units = w_gate.shape
    mine = w_query.shape[1]
    pairs = mine // SLOT
    gain_a, gain_f = attention_norm_gain[None, :], feedforward_norm_gain[None, :]

    outer, inner = split if split else (0, 0)
    me = (lax.axis_index("hi") * lax.axis_size("lo") + lax.axis_index("lo"))[None].astype(jnp.int32)
    tokens_par = swap(tokens)
    qkv_shard = jnp.concatenate(
        [
            w[:, p * SLOT : (p + 1) * SLOT]
            for p in range(pairs)
            for w in (w_query, w_key, w_value)
        ],
        axis=1,
    )
    at_up, at_down, at_out = units, 2 * units, 3 * units
    columns = at_out + mine
    w_rest = gather_rows(jnp.concatenate([w_gate, w_up, w_down.T, w_out.T], axis=1))
    if split:
        pieces = gather_pieces(qkv_shard, split)
    else:
        pieces = [(gather_rows(qkv_shard)[None], [0], 0)]
    cosine, sine, ext_q, ext_k = row_tables(block_seq, block_len, lax.axis_index("mp"))

    query, keys, values, w_qkv, tokens_t = project_qkv(
        me if split else me * 0, tokens, tokens_par, pieces, cosine, sine, ext_q, ext_k
    )
    context, mixed, query = attend(query, keys, values)
    rows = tokens.shape[0]
    context_got = swap(context[rows:])
    w_rest, context_got = tie(w_rest, context_got)
    out_other, w_rest = tie(swap(w_rest[:, at_out:]), w_rest)
    w_other = swap(w_rest)
    xhat_a, inverse_a, hidden, hidden_t = attention_out(
        context, context_got, w_rest, out_other, at_out, tokens, gain_a
    )
    act, da, db, branch = forward_first(hidden, w_rest, units)
    output, part, grad_branch, grad_branch_t, sum_f, sent = forward_and_back(
        hidden, hidden_t, w_other, units, branch, xhat_a, cotangent, gain_a, gain_f
    )

    got = swap(sent)
    grad_gate, grad_up, residual, grad_attn_t, grad_context, grad_context_send, sum_a = backward(
        grad_branch,
        w_rest,
        da,
        db,
        part,
        (xhat_a, inverse_a, gain_a, w_rest, out_other),
        at_out,
    )
    grad_context_par = swap(grad_context_send)
    grad_attn_par = swap(grad_attn_t)
    tile = 768 if units % 768 == 0 else SLOT
    grads_rest = dense_grad(
        lax.axis_index("hi")[None].astype(jnp.int32),
        [
            (hidden_t, grad_gate, 0, units),
            (hidden_t, grad_up, 0, units),
            (grad_branch_t, act, 0, units),
        ],
        tile,
        split,
        got,
    )
    order = split

    def back(pair, query):
        return attend_back(
            pair, query, keys, values, grad_context, grad_context_par, mixed, cosine, sine
        )

    def qkv_grad(pieces, columns):
        grads = None
        for p, piece in enumerate(pieces):
            grads = weight_grad(
                order, me, (tokens_t, 0), (tokens_t, 1), piece, columns, p * 3 * SLOT, grads
            )
        return grads

    gains = jnp.stack([jnp.sum(sum_a, axis=0), jnp.sum(sum_f, axis=0)])
    gains = gains + swap(gains)
    query, grads_rest = tie(query, grads_rest)
    grad_rest = scatter_first(grads_rest, split)
    done = [back(0, query)]
    for pair in range(1, pairs - 1):
        query, done[-1] = tie(query, done[-1])
        done.append(back(pair, query))
    at_late = (pairs - 1) * 3 * SLOT
    early = qkv_grad(done, at_late + mine)
    early = weight_grad(
        order, me, (grad_attn_t, 0), (grad_attn_par, 0), context, at_late + mine, at_late, early
    )
    query, early, grad_rest = tie(query, early, grad_rest)
    if split:
        early_got, early_held = send_half(early, "lo", inner, 1, gains)
        rest_got, rest_held = send_half(grad_rest, "hi", outer, 1)
        done.append(back(pairs - 1, query))
        done[-1], early_got, rest_got = tie(done[-1], early_got, rest_got)
        early, gains = take_half(early_got, early_held)
        grad_rest, _ = take_half(rest_got, rest_held)
        early_got, early_held = send_half(early, "lo", inner, 2, gains)
        rest_got, rest_held = send_half(grad_rest, "hi", outer, 2)
        late = qkv_grad(done[-1:], 3 * SLOT)
        late, done[-1] = tie(late, done[-1])
        late_got, late_held = send_half(late, "lo", inner, 1)
        input_par = input_back(done, w_qkv, True)
        input_par, late_got, early_got = tie(input_par, late_got, early_got)
        input_got = swap(input_par)
        late, _ = take_half(late_got, late_held)
        early, gains = take_half(early_got, early_held)
        late_got, late_held = send_half(late, "lo", inner, 2)
        early_got, early_held = send_half(early, "hi", outer, 1, gains)
        input_grad = input_back(done, w_qkv, False, (residual, input_got))
        input_grad, late_got, early_got, rest_got = tie(input_grad, late_got, early_got, rest_got)
        late, _ = take_half(late_got, late_held)
        early, gains = take_half(early_got, early_held)
        grad_rest, _ = take_half(rest_got, rest_held)
        late_got, late_held = send_half(late, "hi", outer, 1)
        early_got, early_held = send_half(early, "hi", outer, 2, gains)
        late, _ = take_half(late_got, late_held)
        early, gains = take_half(early_got, early_held)
        late, _ = take_half(*send_half(late, "hi", outer, 2))
        step = 4
        while step < outer:
            grad_rest, _ = take_half(*send_half(grad_rest, "hi", outer, step))
            early, gains = take_half(*send_half(early, "hi", outer, step, gains))
            late, _ = take_half(*send_half(late, "hi", outer, step))
            step *= 2
        grad_rest, early, late = grad_rest[0], early[0], late[0]
    else:
        gains = sum_everywhere(gains, axes)
        done.append(back(pairs - 1, query))
        late = qkv_grad(done[-1:], 3 * SLOT)
        input_got = swap(input_back(done, w_qkv, True))
        early, late = scatter_first(early, split), scatter_first(late, split)
        input_grad = input_back(done, w_qkv, False, (residual, input_got))
    grad_out = early[:, at_late:].astype(f32)
    grad_qkv = jnp.concatenate([early[:, :at_late], late], axis=1)
    grad_rest = grad_rest.astype(f32)
    grad_qkv = grad_qkv.astype(f32).reshape(depth, pairs, 3, SLOT)
    grad_query, grad_key, grad_value = (
        grad_qkv[:, :, n].reshape(depth, mine) for n in range(3)
    )
    return (
        output,
        input_grad,
        grad_query,
        grad_key,
        grad_value,
        grad_out.T,
        grad_rest[:, :units],
        grad_rest[:, units : 2 * units],
        grad_rest[:, 2 * units :].T,
        gains[0],
        gains[1],
    )


def solution(mesh):
    n_dp, n_mp = mesh.shape["dp"], mesh.shape["mp"]
    inner = 4 if n_dp % 4 == 0 else 1
    outer = n_dp // inner
    fine = Mesh(mesh.devices.reshape(outer, inner, n_mp), ("hi", "lo", "mp"))
    dp = ("hi", "lo")
    rows = P(("hi", "lo", "mp"), None)
    axes = (("mp", n_mp), ("lo", inner), ("hi", outer))

    def layer(*operands):
        width = operands[0].shape[1]
        depth = width // n_dp
        doubling = n_dp & (n_dp - 1) == 0
        split = (outer, inner) if doubling and depth % 16 == 0 and outer >= 4 else None
        return jax.shard_map(
            functools.partial(local, split, axes),
            mesh=fine,
            in_specs=(
                rows,
                P(dp, "mp"),
                P(dp, "mp"),
                P(dp, "mp"),
                P("mp", dp),
                P(dp, "mp"),
                P(dp, "mp"),
                P("mp", dp),
                P(),
                P(),
                P(dp, None),
                P(dp, None),
                rows,
            ),
            out_specs=(
                rows,
                rows,
                P(dp, "mp"),
                P(dp, "mp"),
                P(dp, "mp"),
                P("mp", dp),
                P(dp, "mp"),
                P(dp, "mp"),
                P("mp", dp),
                P(),
                P(),
            ),
            check_vma=False,
        )(*operands)

    return layer
```

```python
import functools
import math

import jax
import jax.numpy as jnp
from jax import lax
from jax.experimental import pallas as pl
from jax.experimental.pallas import tpu as pltpu
from jax.sharding import Mesh
from jax.sharding import PartitionSpec as P

HEAD_DIM = 64
SEQ_MAX = 2048
QLEN = 64
EPS = 1e-05
ROPE_BASE = 1000.0
MASKED = -1e30
SLOT = 128

TAIL = ('weight_grad', 'input_back')
SHARE = 0.2

bf16 = jnp.bfloat16
f32 = jnp.float32

NN = (((1,), (0,)), ((), ()))
NT = (((1,), (1,)), ((), ()))


def dot(left, right, dims=NN):
    return lax.dot_general(left, right, dims, preferred_element_type=f32)


def call(kernel, name, grid, in_specs, out_specs, out_shape, flops, scratch=(), aliases=None, exps=0):
    def run(*operands):
        outs = out_shape if isinstance(out_shape, (list, tuple)) else [out_shape]
        moved = sum(math.prod(o.shape) * o.dtype.itemsize for o in (*operands, *outs))
        share = SHARE if name in TAIL else 1.0
        return pl.pallas_call(
            kernel,
            name=name,
            grid=grid,
            in_specs=in_specs,
            out_specs=out_specs,
            out_shape=out_shape,
            scratch_shapes=list(scratch),
            input_output_aliases=aliases or {},
            cost_estimate=pl.CostEstimate(
                flops=int(flops * share),
                bytes_accessed=int(moved * share),
                transcendentals=int(exps * share),
            ),
            compiler_params=pltpu.CompilerParams(vmem_limit_bytes=60 * 1024 * 1024),
        )(*operands)

    return run


def shape(dims, dtype):
    return jax.ShapeDtypeStruct(dims, dtype)


def whole(dims):
    return pl.BlockSpec(dims, lambda *_: (0,) * len(dims))


def each_piece(total, block, body):
    for start in range(0, total, block):
        body(pl.ds(start, block))


def fetches(pairs, sems):
    return [pltpu.make_async_copy(src, dst, sems.at[n]) for n, (src, dst) in enumerate(pairs)]


def rope(value, cosine, sine, lane):
    half = HEAD_DIM // 2
    lanes = value.shape[-1]
    swapped = jnp.where(
        lane % HEAD_DIM < half,
        pltpu.roll(value, lanes - half, 1),
        pltpu.roll(value, half, 1),
    )
    return value * cosine + swapped * sine


def qkv_kernel(own_blocks, places, me_ref, own_ref, par_ref, *refs):
    piece_refs = refs[: len(places)]
    cos_ref, sin_ref, eq_ref, ek_ref, q_ref, k_ref, v_ref, w_ref, turned_ref = refs[len(places) :]

    @pl.when(pl.program_id(0) == 0)
    def _():
        for piece_ref, (starts, column) in zip(piece_refs, places):
            _, depth, width = piece_ref.shape
            for n, start in enumerate(starts):
                row = pl.multiple_of((start ^ me_ref[0]) * depth, depth)
                w_ref[pl.ds(row, depth), column : column + width] = piece_ref[n]

    rows = jnp.where(pl.program_id(0) < own_blocks, own_ref[...], par_ref[...])
    turned_ref[...] = rows.T
    lane = lax.broadcasted_iota(jnp.int32, (rows.shape[0], SLOT), 1)
    low = lane < HEAD_DIM
    ones = jnp.where((lane >= HEAD_DIM) & (lane < HEAD_DIM + 3), -1.0, 0.0)
    cosine, sine = cos_ref[...], sin_ref[...]
    ext_q, ext_k = eq_ref[...].astype(f32), ek_ref[...].astype(f32)
    for pair in range(q_ref.shape[0] // 2):
        base = pair * 3 * SLOT
        mixed = dot(rows, w_ref[:, base : base + 3 * SLOT])
        query = rope(mixed[:, :SLOT], cosine, sine, lane) * HEAD_DIM**-0.5
        key = rope(mixed[:, SLOT : 2 * SLOT], cosine, sine, lane)
        value = mixed[:, 2 * SLOT :]
        for ref, data, ext in ((q_ref, query, ext_q), (k_ref, key, ext_k), (v_ref, value, ones)):
            ref[2 * pair] = jnp.where(low, data, ext).astype(bf16)
            ref[2 * pair + 1] = jnp.where(low, pltpu.roll(data, HEAD_DIM, 1), ext).astype(bf16)


def project_qkv(me, own, par, pieces, cosine, sine, ext_q, ext_k, block=512):
    rows, width = own.shape
    arrays = [piece[0] for piece in pieces]
    places = [piece[1:] for piece in pieces]
    columns = max(column + array.shape[2] for array, _, column in pieces)
    heads = columns // (3 * HEAD_DIM)
    count = rows // block
    table = pl.BlockSpec((block, SLOT), lambda i: (i, 0))
    out = pl.BlockSpec((heads, block, SLOT), lambda i: (0, i, 0))
    return call(
        functools.partial(qkv_kernel, count, places),
        "project_qkv",
        (2 * count,),
        [
            pl.BlockSpec(memory_space=pltpu.SMEM),
            pl.BlockSpec((block, width), lambda i: (jnp.minimum(i, count - 1), 0)),
            pl.BlockSpec((block, width), lambda i: (jnp.maximum(i - count, 0), 0)),
            *(whole(array.shape) for array in arrays),
            table,
            table,
            table,
            table,
        ],
        [out] * 3 + [whole((width, columns)), pl.BlockSpec((width, block), lambda i: (0, i))],
        [shape((heads, 2 * rows, SLOT), bf16)] * 3
        + [shape((width, columns), bf16), shape((width, 2 * rows), bf16)],
        4 * rows * width * columns,
    )(me, own, par, *arrays, cosine, sine, ext_q, ext_k)


def split_three(value):
    first = value.astype(bf16).astype(f32)
    second = (value - first).astype(bf16).astype(f32)
    return first, second, value - first - second


def attend_kernel(block, q_ref, k_ref, v_ref, ctx_ref, mix_ref, q2_ref):
    lane = lax.broadcasted_iota(jnp.int32, (block, SLOT), 1)
    low = lane < HEAD_DIM
    for piece in range(q_ref.shape[1] // block):
        rows = pl.ds(piece * block, block)
        mixed = []
        for head in range(2):
            query = q_ref[head, rows, :]
            scores = dot(query, k_ref[head], NT)
            peak = jnp.max(scores, axis=-1, keepdims=True)
            expo = jnp.exp(scores - peak).astype(bf16)
            total_mix = dot(expo, v_ref[head])
            total = -total_mix[:, HEAD_DIM : HEAD_DIM + 1]
            mixed.append(total_mix * (1.0 / total))
            parts = split_three(peak + jnp.log(total))
            kept = query.astype(f32)
            for at, part in enumerate(parts):
                kept = jnp.where(lane == HEAD_DIM + 32 + at, part, kept)
            q2_ref[head, rows, :] = kept.astype(bf16)
        both = jnp.where(low, mixed[0], pltpu.roll(mixed[1], HEAD_DIM, 1))
        mix_ref[rows, :] = both
        ctx_ref[rows, :] = both.astype(bf16)


def attend(query, keys, values, block=512, step=1024):
    heads, rows, _ = query.shape
    piece = pl.BlockSpec((2, step, SLOT), lambda p, i: (p, i, 0))
    full = pl.BlockSpec((2, rows, SLOT), lambda p, i: (p, 0, 0))
    out = pl.BlockSpec((step, SLOT), lambda p, i: (i, p))
    width = heads * HEAD_DIM
    return call(
        functools.partial(attend_kernel, block),
        "attend",
        (heads // 2, rows // step),
        [piece, full, full],
        [out, out, piece],
        [shape((rows, width), bf16), shape((rows, width), f32), shape(query.shape, bf16)],
        4 * heads * rows * rows * SLOT,
        exps=heads * rows * rows,
    )(query, keys, values)


def attend_back_kernel(
    unroll, q_ref, k_ref, v_ref, own_ref, par_ref, mix_ref, cos_ref, sin_ref, out_ref, dq_ref, dk_ref, dv_ref
):
    at = pl.program_id(1)
    block, rows = q_ref.shape[1], k_ref.shape[1]
    lane = lax.broadcasted_iota(jnp.int32, (block, SLOT), 1)
    low = lane < HEAD_DIM
    place = pl.ds(pl.multiple_of(at * block, block), block)

    @pl.when(at == 0)
    def _():
        dk_ref[...] = jnp.zeros_like(dk_ref)
        dv_ref[...] = jnp.zeros_like(dv_ref)

    def head_back(head, carry):
        first = at * 2 < pl.num_programs(1)
        grad = jnp.where(first, own_ref[...], par_ref[...]).astype(f32)
        mine = low == (head == 0)
        delta = jnp.sum(jnp.where(mine, grad * mix_ref[...], 0.0), axis=-1, keepdims=True)
        kept = jnp.where(head == 0, grad, pltpu.roll(grad, HEAD_DIM, 1))
        kept = jnp.where(low, kept, 0.0)
        for n, piece in enumerate(split_three(delta)):
            kept = jnp.where(lane == HEAD_DIM + n, piece, kept)
        grad = kept.astype(bf16)
        query, keys = q_ref[head], k_ref[head]
        probs = jnp.exp(dot(query, keys, NT))
        grad_scores = (probs * dot(grad, v_ref[head], NT)).astype(bf16)
        dv_ref[head] += dot(grad.T, probs.astype(bf16))
        dk_ref[head] += dot(query.T, grad_scores)
        dq_ref[head] = dot(grad_scores, keys)
        return carry

    lax.fori_loop(0, 2, head_back, 0, unroll=unroll)
    grad_query = jnp.where(low, dq_ref[0], pltpu.roll(dq_ref[1], HEAD_DIM, 1))
    turned = rope(grad_query, cos_ref[place, :], -sin_ref[place, :], lane)
    out_ref[place, :SLOT] = (turned * HEAD_DIM**-0.5).astype(bf16)

    @pl.when(at == pl.num_programs(1) - 1)
    def _():
        def write(n, carry):
            span = pl.ds(pl.multiple_of(n * block, block), block)
            grad_key, grad_value = (
                jnp.where(low, ref[0, :, span].T, pltpu.roll(ref[1, :, span].T, HEAD_DIM, 1))
                for ref in (dk_ref, dv_ref)
            )
            grad_key = rope(grad_key, cos_ref[span, :], -sin_ref[span, :], lane)
            out_ref[span, SLOT : 2 * SLOT] = grad_key.astype(bf16)
            out_ref[span, 2 * SLOT :] = grad_value.astype(bf16)
            return carry

        lax.fori_loop(0, rows // block, write, 0)


def attend_back(first, pairs, query, keys, values, own, par, mixed, cosine, sine, block=512, unroll=True):
    heads, rows, _ = query.shape
    half = own.shape[0]
    count = half // block
    full = pl.BlockSpec((2, rows, SLOT), lambda p, i: (first + p, 0, 0))
    return call(
        functools.partial(attend_back_kernel, unroll),
        "attend_back",
        (pairs, rows // block),
        [
            pl.BlockSpec((2, block, SLOT), lambda p, i: (first + p, i, 0)),
            full,
            full,
            pl.BlockSpec((block, SLOT), lambda p, i: (jnp.minimum(i, count - 1), first + p)),
            pl.BlockSpec((block, SLOT), lambda p, i: (jnp.maximum(i - count, 0), first + p)),
            pl.BlockSpec((block, SLOT), lambda p, i: (i, first + p)),
            whole((rows, SLOT)),
            whole((rows, SLOT)),
        ],
        pl.BlockSpec((rows, 3 * SLOT), lambda p, i: (0, p)),
        shape((rows, pairs * 3 * SLOT), bf16),
        10 * 2 * pairs * rows * rows * SLOT,
        scratch=[pltpu.VMEM((2, block, SLOT), f32)] + [pltpu.VMEM((2, SLOT, rows), f32)] * 2,
        exps=2 * pairs * rows * rows,
    )(query, keys, values, own, par, mixed, cosine, sine)


def normalize(value):
    mean = jnp.mean(value, axis=-1, keepdims=True)
    centred = value - mean
    inverse = lax.rsqrt(jnp.mean(centred * centred, axis=-1, keepdims=True) + EPS)
    return centred * inverse, inverse


def normalize_back(grad, xhat, inverse, gain):
    scaled = grad * gain
    return inverse * (
        scaled
        - jnp.mean(scaled, axis=-1, keepdims=True)
        - xhat * jnp.mean(scaled * xhat, axis=-1, keepdims=True)
    )


def fold_rows(value):
    return jnp.sum(value.reshape(-1, 8, value.shape[-1]), axis=0)


def attention_out_kernel(
    ctx_ref, got_ref, mine_ref, other_ref, tok_ref, gain_ref, xhat_ref, inv_ref, low_ref, turned_ref
):
    branch = dot(ctx_ref[...], mine_ref[...], NT) + dot(got_ref[...], other_ref[...], NT)
    xhat, inverse = normalize(tok_ref[...].astype(f32) + branch)
    xhat_ref[...] = xhat
    inv_ref[...] = inverse
    low = (xhat * gain_ref[...]).astype(bf16)
    low_ref[...] = low
    turned_ref[...] = low.T


def attention_out(ctx, got, mine, other, at, tokens, gain, block=256):
    rows, width = tokens.shape
    half = got.shape[1]
    piece = pl.BlockSpec((block, half), lambda i: (i, 0))
    row = pl.BlockSpec((block, width), lambda i: (i, 0))
    return call(
        attention_out_kernel,
        "attention_out",
        (rows // block,),
        [
            piece,
            piece,
            pl.BlockSpec((width, half), lambda i: (0, at // half)),
            whole(other.shape),
            row,
            whole((1, width)),
        ],
        [
            row,
            pl.BlockSpec((block, 1), lambda i: (i, 0)),
            row,
            pl.BlockSpec((width, block), lambda i: (0, i)),
        ],
        [
            shape((rows, width), f32),
            shape((rows, 1), f32),
            shape((rows, width), bf16),
            shape((width, rows), bf16),
        ],
        4 * rows * width * half,
    )(ctx, got, mine, other, tokens, gain)


def gate_up_tile(x_ref, gate_ref, up_ref, down_ref, act_ref, da_ref, db_ref, acc_ref, block):
    def body(span):
        gate = dot(x_ref[span, :], gate_ref[...])
        up = dot(x_ref[span, :], up_ref[...])
        sigma = jax.nn.sigmoid(gate)
        swish = gate * sigma
        act = (swish * up).astype(bf16)
        act_ref[span, :] = act
        da_ref[span, :] = (up * (sigma * (1.0 + gate * (1.0 - sigma)))).astype(bf16)
        db_ref[span, :] = swish.astype(bf16)
        acc_ref[span, :] += dot(act, down_ref[...], NT)

    each_piece(x_ref.shape[0], block, body)


def forward_first_kernel(block, x_ref, gate_ref, up_ref, down_ref, act_ref, da_ref, db_ref, acc_ref):
    @pl.when(pl.program_id(0) == 0)
    def _():
        acc_ref[...] = jnp.zeros_like(acc_ref)

    gate_up_tile(
        x_ref, gate_ref, up_ref, down_ref, act_ref, da_ref, db_ref, acc_ref, block
    )


def forward_first(x, weights, units, tile=512, block=1024):
    rows, width = x.shape
    count = units // tile
    out = pl.BlockSpec((rows, tile), lambda n: (0, n))
    return call(
        functools.partial(forward_first_kernel, block),
        "forward_first",
        (count,),
        [whole((rows, width))]
        + [pl.BlockSpec((width, tile), lambda n, at=at: (0, at * count + n)) for at in range(3)],
        [out] * 3 + [whole((rows, width))],
        [shape((rows, units), bf16)] * 3 + [shape((rows, width), f32)],
        6 * rows * width * units,
    )(x, weights, weights, weights)


def turn_kernel(
    block,
    count,
    x_ref,
    gate_w_ref,
    up_w_ref,
    down_w_ref,
    gain_a_ref,
    gain_f_ref,
    part_src,
    xhat_src,
    cot_src,
    xt_src,
    out_ref,
    mid_ref,
    low_ref,
    turned_ref,
    sum_ref,
    grads_ref,
    act_ref,
    da_ref,
    db_ref,
    grad_ref,
    acc_ref,
    part_ref,
    xhat_ref,
    cot_ref,
    xt_ref,
    sems,
):
    at = pl.program_id(0)
    copies = fetches(
        [(part_src, part_ref), (xhat_src, xhat_ref), (cot_src, cot_ref), (xt_src, xt_ref)], sems
    )

    @pl.when(at == 0)
    def _():
        acc_ref[...] = jnp.zeros_like(acc_ref)
        for copy in copies:
            copy.start()

    @pl.when(at < count)
    def _():
        gate_up_tile(
            x_ref,
            gate_w_ref,
            up_w_ref,
            down_w_ref,
            act_ref.at[at],
            da_ref.at[at],
            db_ref.at[at],
            acc_ref,
            block,
        )

    @pl.when(at == count - 1)
    def _():
        for copy in copies:
            copy.wait()
        gain_a, gain_f = gain_a_ref[...], gain_f_ref[...]
        sum_ref[...] = jnp.zeros_like(sum_ref)

        def body(span):
            branch = part_ref[span, :] + acc_ref[span, :]
            xhat, inverse = normalize(xhat_ref[span, :] * gain_a + branch)
            out_ref[span, :] = (xhat * gain_f).astype(bf16)
            grad = cot_ref[span, :].astype(f32)
            middle = normalize_back(grad, xhat, inverse, gain_f)
            mid_ref[span, :] = middle
            low = middle.astype(bf16)
            low_ref[span, :] = low
            turned_ref[:, span] = low.T
            sum_ref[...] += fold_rows(grad * xhat)

        each_piece(x_ref.shape[0], 256, body)

    @pl.when(at >= count)
    def _():
        tile = at - count

        def body(span):
            grad = dot(low_ref[span, :], down_w_ref[...])
            gate = (grad * da_ref[tile, span, :].astype(f32)).astype(bf16)
            up = (grad * db_ref[tile, span, :].astype(f32)).astype(bf16)
            grad_ref[0, span, :] = gate
            grad_ref[1, span, :] = up
            mid_ref[span, :] += dot(gate, gate_w_ref[...], NT) + dot(up, up_w_ref[...], NT)

        each_piece(x_ref.shape[0], 512, body)
        grads_ref[0] = dot(xt_ref[...], grad_ref[0]).astype(bf16)
        grads_ref[1] = dot(xt_ref[...], grad_ref[1]).astype(bf16)
        grads_ref[2] = dot(turned_ref[...], act_ref[tile]).astype(bf16)


def forward_and_back(x, turned, weights, units, part, xhat, cotangent, gain_a, gain_f, tile=512, block=1024):
    rows, width = x.shape
    count = units // tile
    full, gain = whole((rows, width)), whole((1, width))
    flat = whole((width, rows))

    def weight(part):
        return pl.BlockSpec((width, tile), lambda n: (0, part * count + lax.rem(n, count)))

    return call(
        functools.partial(turn_kernel, block, count),
        "forward_and_back",
        (2 * count,),
        [full, weight(0), weight(1), weight(2), gain, gain] + [pl.BlockSpec(memory_space=pl.ANY)] * 4,
        [
            full,
            full,
            full,
            flat,
            whole((8, width)),
            pl.BlockSpec((3, width, tile), lambda n: (0, 0, jnp.maximum(n - count, 0))),
        ],
        [
            shape((rows, width), bf16),
            shape((rows, width), f32),
            shape((rows, width), bf16),
            shape((width, rows), bf16),
            shape((8, width), f32),
            shape((3, width, units), bf16),
        ],
        18 * rows * width * units,
        scratch=[pltpu.VMEM((count, rows, tile), bf16)] * 3
        + [pltpu.VMEM((2, rows, tile), bf16)]
        + [pltpu.VMEM((rows, width), f32)] * 3
        + [
            pltpu.VMEM((rows, width), bf16),
            pltpu.VMEM((width, rows), bf16),
            pltpu.SemaphoreType.DMA((4,)),
        ],
    )(x, weights, weights, weights, gain_a, gain_f, part, xhat, cotangent, turned)


def backward_kernel(
    block,
    g_ref,
    gate_w_ref,
    up_w_ref,
    down_w_ref,
    da_ref,
    db_ref,
    part_src,
    xhat_src,
    inv_ref,
    gain_ref,
    mine_ref,
    other_ref,
    gate_ref,
    up_ref,
    res_ref,
    turned_ref,
    keep_ref,
    send_ref,
    sum_ref,
    acc_ref,
    part_ref,
    xhat_ref,
    sems,
):
    copies = fetches([(part_src, part_ref), (xhat_src, xhat_ref)], sems)

    @pl.when(pl.program_id(0) == 0)
    def _():
        acc_ref[...] = jnp.zeros_like(acc_ref)
        for copy in copies:
            copy.start()

    def tile(span):
        grad = dot(g_ref[span, :], down_w_ref[...])
        gate = (grad * da_ref[span, :].astype(f32)).astype(bf16)
        up = (grad * db_ref[span, :].astype(f32)).astype(bf16)
        gate_ref[span, :] = gate
        up_ref[span, :] = up
        acc_ref[span, :] += dot(gate, gate_w_ref[...], NT) + dot(up, up_w_ref[...], NT)

    each_piece(g_ref.shape[0], block, tile)

    @pl.when(pl.program_id(0) == pl.num_programs(0) - 1)
    def _():
        for copy in copies:
            copy.wait()
        gain = gain_ref[...]
        sum_ref[...] = jnp.zeros_like(sum_ref)

        def body(span):
            grad, xhat = acc_ref[span, :] + part_ref[span, :], xhat_ref[span, :]
            residual = normalize_back(grad, xhat, inv_ref[span, :], gain)
            res_ref[span, :] = residual
            low = residual.astype(bf16)
            turned_ref[:, span] = low.T
            keep_ref[span, :] = dot(low, mine_ref[...]).astype(bf16)
            send_ref[span, :] = dot(low, other_ref[...]).astype(bf16)
            sum_ref[...] += fold_rows(grad * xhat)

        each_piece(g_ref.shape[0], 256, body)


def backward(grad, weights, da, db, part, xhat, inverse, gain, out_other, at, tile=512, block=512):
    rows, width = grad.shape
    units, half = da.shape[1], out_other.shape[1]
    count = units // tile
    full = whole((rows, width))
    out = pl.BlockSpec((rows, tile), lambda n: (0, n))
    late = pl.BlockSpec(memory_space=pl.ANY)
    part_out = whole((rows, half))
    return call(
        functools.partial(backward_kernel, block),
        "backward",
        (count,),
        [
            full,
            *(pl.BlockSpec((width, tile), lambda n, p=p: (0, p * count + n)) for p in range(3)),
            out,
            out,
            late,
            late,
            whole((rows, 1)),
            whole((1, width)),
            pl.BlockSpec((width, half), lambda n: (0, at // half)),
            whole((width, half)),
        ],
        [out, out, full, whole((width, rows)), part_out, part_out, whole((8, width))],
        [shape((rows, units), bf16)] * 2
        + [
            shape((rows, width), f32),
            shape((width, rows), bf16),
            shape((rows, half), bf16),
            shape((rows, half), bf16),
            shape((8, width), f32),
        ],
        6 * rows * width * units + 4 * rows * width * half,
        scratch=[pltpu.VMEM((rows, width), f32)] * 3 + [pltpu.SemaphoreType.DMA((2,))],
    )(grad, weights, weights, weights, da, db, part, xhat, inverse, gain, weights, out_other)


def mirrored(index, count):
    bits = count.bit_length() - 1
    return sum(((index >> bit) & 1) << (bits - 1 - bit) for bit in range(bits))


def weight_grad_kernel(order, crossed, tiles, me_ref, *refs):
    *refs, out_ref = refs
    at = pl.program_id(0)
    first = 0
    for n, steps in enumerate(tiles):
        own_ref, par_ref, yo_ref, yp_ref = refs[4 * n : 4 * n + 4]

        def write(own_ref=own_ref, par_ref=par_ref, yo_ref=yo_ref, yp_ref=yp_ref):
            total = dot(own_ref[...], yo_ref[...]) + dot(par_ref[...], yp_ref[...])
            total = total.astype(bf16)
            if order is None:
                out_ref[...] = total
                return
            count = math.prod(order)
            depth = total.shape[0] // count
            for shard in range(count):
                apart = shard ^ me_ref[0]
                if crossed:
                    apart = (apart & (count - 4)) | ((apart & 1) << 1) | ((apart >> 1) & 1)
                out_ref[mirrored(apart, count)] = total[shard * depth : (shard + 1) * depth]

        pl.when((at >= first) & (at < first + steps))(write)
        first += steps


def weight_grad(order, me, segments, tile, crossed=False):
    rows = segments[0][2].shape[0] // 2
    width = segments[0][0][0].shape[0]
    tiles = [n // tile for *_, n in segments]
    columns = sum(tiles) * tile
    operands, specs = [me], [pl.BlockSpec(memory_space=pltpu.SMEM)]
    for n, (own, par, grad, start, _) in enumerate(segments):
        operands += [own[0], par[0], grad, grad]
        specs += [
            pl.BlockSpec((width, rows), lambda i, at=at: (0, at)) for at in (own[1], par[1])
        ]

        def column(i, first=sum(tiles[:n]), last=tiles[n] - 1, source=start // tile):
            return source + jnp.clip(i - first, 0, last)

        specs += [
            pl.BlockSpec((rows, tile), lambda i, half=half, column=column: (half, column(i)))
            for half in range(2)
        ]
    if order:
        count = math.prod(order)
        dims = (count, width // count, columns)
        out = pl.BlockSpec((*dims[:2], tile), lambda i: (0, 0, i))
    else:
        dims = (width, columns)
        out = pl.BlockSpec((width, tile), lambda i: (0, i))
    return call(
        functools.partial(weight_grad_kernel, order, crossed, tiles),
        "weight_grad",
        (sum(tiles),),
        specs,
        out,
        shape(dims, bf16),
        4 * rows * width * columns,
    )(*operands)


def dense_grad_kernel(outer, inner, tiles, add, hi_ref, *refs):
    segments = len(tiles)
    row_refs, grad_refs, refs = refs[:segments], refs[segments : 2 * segments], refs[2 * segments :]
    out_ref = refs[-1]
    at = pl.program_id(0)
    first = 0
    for row_ref, grad_ref, count in zip(row_refs, grad_refs, tiles):

        def write(row_ref=row_ref, grad_ref=grad_ref):
            total = dot(row_ref[...], grad_ref[...])
            if add:
                total = total + refs[0][0].astype(f32)
            total = total.astype(bf16)
            if outer is None:
                out_ref[...] = total
            else:
                depth = total.shape[0] // (outer * inner)
                for hi in range(outer):
                    place = mirrored(hi ^ hi_ref[0], outer)
                    for lo in range(inner):
                        start = (hi * inner + lo) * depth
                        out_ref[lo, place] = total[start : start + depth]

        pl.when((at >= first) & (at < first + count))(write)
        first += count


def dense_grad(me_hi, segments, tile, split=None, add=None):
    width, rows = segments[0][0].shape
    tiles = [columns // tile for *_, columns in segments]
    columns = sum(tiles) * tile
    starts = [sum(tiles[:n]) for n in range(len(tiles))]

    def spec(at, start, count):
        return pl.BlockSpec((rows, tile), lambda i: (0, at // tile + jnp.clip(i - start, 0, count - 1)))

    operands = [me_hi] + [x for x, *_ in segments] + [y for _, y, *_ in segments]
    specs = [pl.BlockSpec(memory_space=pltpu.SMEM)] + [whole((width, rows)) for _ in segments]
    specs += [spec(at, start, n) for (_, _, at, _), start, n in zip(segments, starts, tiles)]
    flat = pl.BlockSpec((width, tile), lambda i: (0, i))
    if add is not None:
        operands.append(add)
        per = add.shape[2] // tile
        specs.append(pl.BlockSpec((1, width, tile), lambda i: (i // per, 0, lax.rem(i, per))))
    outer, inner = split if split else (None, None)
    if split:
        dims = (inner, outer, width // (outer * inner), columns)
        out = pl.BlockSpec((*dims[:3], tile), lambda i: (0, 0, 0, i))
    else:
        dims, out = (width, columns), flat
    return call(
        functools.partial(dense_grad_kernel, outer, inner, tiles, add is not None),
        "dense_grad",
        (columns // tile,),
        specs,
        out,
        shape(dims, bf16),
        2 * rows * width * columns,
    )(*operands)


def input_back_kernel(*refs):
    *piece_refs, w_ref, out_ref = refs
    joined = jnp.concatenate([ref[...] for ref in piece_refs], axis=1)
    out_ref[...] = dot(joined, w_ref[...], NT).astype(bf16)


def input_back_add_kernel(*refs):
    *piece_refs, w_ref, res_ref, got_ref, out_ref = refs
    joined = jnp.concatenate([ref[...] for ref in piece_refs], axis=1)
    total = dot(joined, w_ref[...], NT) + res_ref[...] + got_ref[...].astype(f32)
    out_ref[...] = total.astype(bf16)


def input_back(pieces, weights, lower, extra=(), block=256):
    rows = pieces[0].shape[0] // 2
    width, columns = weights.shape
    count = rows // block
    first = count if lower else 0
    row = pl.BlockSpec((block, width), lambda i: (i, 0))
    return call(
        input_back_add_kernel if extra else input_back_kernel,
        "input_back",
        (count,),
        [pl.BlockSpec((block, p.shape[1]), lambda i: (first + i, 0)) for p in pieces]
        + [whole(weights.shape)]
        + [row] * len(extra),
        row,
        shape((rows, width), bf16),
        2 * rows * width * columns,
    )(*pieces, weights, *extra)


def swap(value):
    return lax.ppermute(value, "mp", [(0, 1), (1, 0)])


def sum_everywhere(value, axes):
    for axis, size in axes:
        if size & (size - 1):
            return lax.psum(value, tuple(name for name, _ in axes))
    for axis, size in axes:
        step = 1
        while step < size:
            value = value + lax.ppermute(value, axis, [(i, i ^ step) for i in range(size)])
            step *= 2
    return value


def exchange(value, axis, size, step):
    return lax.ppermute(value, axis, [(i, i ^ step) for i in range(size)])


def gather_rows(shard):
    return lax.all_gather(shard, ("hi", "lo"), axis=0, tiled=True)


def gather_pieces(shard, split):
    outer, inner = split
    held = shard[None]
    step = outer // 2
    starts = [0]
    while step:
        held = jnp.concatenate([held, exchange(held, "hi", outer, step)])
        starts = starts + [start ^ (step * inner) for start in starts]
        step //= 2
    cut = shard.shape[1] // (2 * SLOT) * SLOT
    pieces = [(held, starts, 0)]
    for column, width, bits in ((0, cut, (1, 2)), (cut, shard.shape[1] - cut, (2, 1))):
        part = lax.slice_in_dim(held, column, column + width, axis=2)
        once = exchange(part, "lo", inner, bits[0])
        twice = exchange(jnp.concatenate([part, once]), "lo", inner, bits[1])
        beside = [start ^ bits[0] for start in starts]
        pieces.append((once, beside, column))
        pieces.append((twice, [start ^ bits[1] for start in starts + beside], column))
    return pieces


def scatter_first(partial, split):
    if not split:
        return lax.psum_scatter(partial, ("hi", "lo"), scatter_dimension=0, tiled=True)
    return lax.psum_scatter(partial, "lo", scatter_dimension=0, tiled=False)


def to_terms(value, columns):
    terms = jnp.stack([term.astype(bf16) for term in split_three(value)])
    whole_rows = 16 * columns
    flat = terms.reshape(-1)
    return jnp.pad(flat, (0, -flat.size % whole_rows)).reshape(-1, columns)


def from_terms(rows, dims):
    count = 3 * math.prod(dims)
    return jnp.sum(rows.reshape(-1)[:count].reshape(3, *dims).astype(f32), axis=0)


def send_half(partial, axis, size, step, rider=None):
    half, (depth, columns) = partial.shape[0] // 2, partial.shape[1:]
    message = partial[half:].reshape(half * depth, columns)
    terms = None
    if rider is not None:
        terms = to_terms(rider, columns)
        message = jnp.concatenate([message, terms])
        rider = from_terms(terms, rider.shape)
    return exchange(message, axis, size, step), (partial[:half], rider)


def take_half(got, held):
    kept, rider = held
    rows = kept.shape[0] * kept.shape[1]
    if rider is not None:
        rider = rider + from_terms(got[rows:], rider.shape)
        got = got[:rows]
    return (kept.astype(f32) + got.reshape(kept.shape).astype(f32)).astype(bf16), rider


def tie(*values):
    return lax.optimization_barrier(values)


def row_tables(block_seq, block_len, core):
    blocks = SEQ_MAX // QLEN
    sequence, lengths = block_seq.reshape(blocks), block_len.reshape(blocks)
    index = jnp.arange(blocks, dtype=jnp.int32)
    same = sequence[:, None] == sequence[None, :]
    first = jnp.min(jnp.where(same, index[None, :], blocks), axis=1)
    table = jnp.stack([sequence, lengths, QLEN * (index - first)])
    turned = jnp.concatenate([table[:, blocks // 2 :], table[:, : blocks // 2]], axis=1)
    table = jnp.where(core == 0, table, turned)
    sequence, lengths, start = (jnp.repeat(part, QLEN)[:, None] for part in table)
    inside = (jnp.arange(SEQ_MAX, dtype=jnp.int32) % QLEN)[:, None]
    position = (start + inside).astype(f32)
    valid = inside < lengths

    lane = jnp.arange(SLOT, dtype=jnp.int32)
    half = HEAD_DIM // 2
    inverse = jnp.exp((lane % half).astype(f32) * (-2.0 * math.log(ROPE_BASE) / HEAD_DIM))
    angle = position * inverse[None, :]
    cosine = jnp.cos(angle)
    sine = jnp.sin(angle) * jnp.where(lane % HEAD_DIM < half, -1.0, 1.0)[None, :]

    column = (lane - HEAD_DIM)[None, :]
    in_mask = (column >= 0) & (column < blocks)
    match = column == sequence
    ext_q = jnp.where(in_mask & match, 1.0, 0.0).astype(bf16)
    ext_k = jnp.where(
        in_mask,
        jnp.where(match & valid, 0.0, MASKED),
        jnp.where((column >= 32) & (column < 35), -1.0, 0.0),
    ).astype(bf16)
    return cosine, sine, ext_q, ext_k


def local(
    split,
    axes,
    tokens,
    w_query,
    w_key,
    w_value,
    w_out,
    w_gate,
    w_up,
    w_down,
    attention_norm_gain,
    feedforward_norm_gain,
    block_seq,
    block_len,
    cotangent,
):
    depth, units = w_gate.shape
    mine = w_query.shape[1]
    pairs = mine // SLOT
    gain_a, gain_f = attention_norm_gain[None, :], feedforward_norm_gain[None, :]

    outer, inner = split if split else (0, 0)
    me = (lax.axis_index("hi") * lax.axis_size("lo") + lax.axis_index("lo"))[None].astype(jnp.int32)
    tokens_par = swap(tokens)
    qkv_shard = jnp.concatenate(
        [
            w[:, p * SLOT : (p + 1) * SLOT]
            for p in range(pairs)
            for w in (w_query, w_key, w_value)
        ],
        axis=1,
    )
    at_up, at_down, at_out = units, 2 * units, 3 * units
    columns = at_out + mine
    w_rest = gather_rows(jnp.concatenate([w_gate, w_up, w_down.T, w_out.T], axis=1))
    if split:
        pieces = gather_pieces(qkv_shard, split)
    else:
        pieces = [(gather_rows(qkv_shard)[None], [0], 0)]
    cosine, sine, ext_q, ext_k = row_tables(block_seq, block_len, lax.axis_index("mp"))

    query, keys, values, w_qkv, tokens_t = project_qkv(
        me if split else me * 0, tokens, tokens_par, pieces, cosine, sine, ext_q, ext_k
    )
    context, mixed, query = attend(query, keys, values)
    rows = tokens.shape[0]
    context_got = swap(context[rows:])
    w_rest, context_got = tie(w_rest, context_got)
    out_other, w_rest = tie(swap(w_rest[:, at_out:]), w_rest)
    w_other = swap(w_rest)
    xhat_a, inverse_a, hidden, hidden_t = attention_out(
        context, context_got, w_rest, out_other, at_out, tokens, gain_a
    )
    act, da, db, branch = forward_first(hidden, w_rest, units)
    output, part, grad_branch, grad_branch_t, sum_f, sent = forward_and_back(
        hidden, hidden_t, w_other, units, branch, xhat_a, cotangent, gain_a, gain_f
    )

    got = swap(sent)
    grad_gate, grad_up, residual, grad_attn_t, grad_context, grad_context_send, sum_a = backward(
        grad_branch, w_rest, da, db, part, xhat_a, inverse_a, gain_a, out_other, at_out
    )
    grad_context_par = swap(grad_context_send)
    grad_attn_par = swap(grad_attn_t)
    tile = 768 if units % 768 == 0 else SLOT
    grads_rest = dense_grad(
        lax.axis_index("hi")[None].astype(jnp.int32),
        [
            (hidden_t, grad_gate, 0, units),
            (hidden_t, grad_up, 0, units),
            (grad_branch_t, act, 0, units),
        ],
        tile,
        split,
        got,
    )
    order = split

    gains = jnp.stack([jnp.sum(sum_a, axis=0), jnp.sum(sum_f, axis=0)])
    gains = gains + swap(gains)
    query, grads_rest = tie(query, grads_rest)
    grad_rest = scatter_first(grads_rest, split)
    done = attend_back(
        0, pairs, query, keys, values, grad_context, grad_context_par, mixed, cosine, sine
    )
    done, grad_rest = tie(done, grad_rest)
    each = 3 * SLOT
    cut = (pairs - 1) * each
    turned = ((tokens_t, 0), (tokens_t, 1))
    if split:
        rest_got, rest_held = send_half(grad_rest, "hi", outer, 1)
    early = weight_grad(order, me, [(*turned, done, 0, cut)], each)
    early, done = tie(early, done)
    if split:
        early_got, early_held = send_half(early, "lo", inner, 1, gains)
    late = weight_grad(
        order,
        me,
        [
            (*turned, done, cut, each),
            ((grad_attn_t, 0), (grad_attn_par, 0), context, 0, mine),
        ],
        each,
        crossed=True,
    )
    if split:
        late, done, rest_got = tie(late, done, rest_got)
        grad_rest, _ = take_half(rest_got, rest_held)
        rest_got, rest_held = send_half(grad_rest, "hi", outer, 2)
        late_got, late_held = send_half(late, "lo", inner, 2)
        input_par = input_back([done], w_qkv, True)
        input_par, early_got, late_got = tie(input_par, early_got, late_got)
        input_got = swap(input_par)
        early, gains = take_half(early_got, early_held)
        early_got, early_held = send_half(early, "lo", inner, 2, gains)
        late, _ = take_half(late_got, late_held)
        late_got, late_held = send_half(late, "lo", inner, 1)
        input_grad = input_back([done], w_qkv, False, (residual, input_got))
        input_grad, late_got, early_got, rest_got = tie(input_grad, late_got, early_got, rest_got)
        early, gains = take_half(early_got, early_held)
        late, _ = take_half(late_got, late_held)
        both = jnp.concatenate([early, late], axis=2)
        both_got, both_held = send_half(both, "hi", outer, 1, gains)
        grad_rest, _ = take_half(rest_got, rest_held)
        both, gains = take_half(both_got, both_held)
        step = 2
        while step < outer:
            both, gains = take_half(*send_half(both, "hi", outer, step, gains))
            if step > 2:
                grad_rest, _ = take_half(*send_half(grad_rest, "hi", outer, step))
            step *= 2
        grad_rest, both = grad_rest[0], both[0]
    else:
        gains = sum_everywhere(gains, axes)
        both = scatter_first(jnp.concatenate([early, late], axis=1), split)
        late, done = tie(late, done)
        input_got = swap(input_back([done], w_qkv, True))
        input_grad = input_back([done], w_qkv, False, (residual, input_got))
    grad_out = both[:, cut + each :].astype(f32)
    grad_qkv = both[:, : cut + each]
    grad_rest = grad_rest.astype(f32)
    grad_qkv = grad_qkv.astype(f32).reshape(depth, pairs, 3, SLOT)
    grad_query, grad_key, grad_value = (
        grad_qkv[:, :, n].reshape(depth, mine) for n in range(3)
    )
    return (
        output,
        input_grad,
        grad_query,
        grad_key,
        grad_value,
        grad_out.T,
        grad_rest[:, :units],
        grad_rest[:, units : 2 * units],
        grad_rest[:, 2 * units :].T,
        gains[0],
        gains[1],
    )


def solution(mesh):
    n_dp, n_mp = mesh.shape["dp"], mesh.shape["mp"]
    inner = 4 if n_dp % 4 == 0 else 1
    outer = n_dp // inner
    fine = Mesh(mesh.devices.reshape(outer, inner, n_mp), ("hi", "lo", "mp"))
    dp = ("hi", "lo")
    rows = P(("hi", "lo", "mp"), None)
    axes = (("mp", n_mp), ("lo", inner), ("hi", outer))

    def layer(*operands):
        width = operands[0].shape[1]
        depth = width // n_dp
        doubling = n_dp & (n_dp - 1) == 0
        split = (outer, inner) if doubling and depth % 16 == 0 and outer >= 4 else None
        return jax.shard_map(
            functools.partial(local, split, axes),
            mesh=fine,
            in_specs=(
                rows,
                P(dp, "mp"),
                P(dp, "mp"),
                P(dp, "mp"),
                P("mp", dp),
                P(dp, "mp"),
                P(dp, "mp"),
                P("mp", dp),
                P(),
                P(),
                P(dp, None),
                P(dp, None),
                rows,
            ),
            out_specs=(
                rows,
                rows,
                P(dp, "mp"),
                P(dp, "mp"),
                P(dp, "mp"),
                P("mp", dp),
                P(dp, "mp"),
                P(dp, "mp"),
                P("mp", dp),
                P(),
                P(),
            ),
            check_vma=False,
        )(*operands)

    return layer
```

```python
import functools
import math

import jax
import jax.numpy as jnp
from jax import lax
from jax.experimental import pallas as pl
from jax.experimental.pallas import tpu as pltpu
from jax.sharding import Mesh
from jax.sharding import PartitionSpec as P

HEAD_DIM = 64
SEQ_MAX = 2048
QLEN = 64
EPS = 1e-05
ROPE_BASE = 1000.0
MASKED = -1e30
SLOT = 128

TAIL = ('weight_grad', 'input_back')
SHARE = 0.05

bf16 = jnp.bfloat16
f32 = jnp.float32

NN = (((1,), (0,)), ((), ()))
NT = (((1,), (1,)), ((), ()))


def dot(left, right, dims=NN):
    return lax.dot_general(left, right, dims, preferred_element_type=f32)


def call(kernel, name, grid, in_specs, out_specs, out_shape, flops, scratch=(), aliases=None, exps=0):
    def run(*operands):
        outs = out_shape if isinstance(out_shape, (list, tuple)) else [out_shape]
        moved = sum(math.prod(o.shape) * o.dtype.itemsize for o in (*operands, *outs))
        share = SHARE if name in TAIL else 1.0
        return pl.pallas_call(
            kernel,
            name=name,
            grid=grid,
            in_specs=in_specs,
            out_specs=out_specs,
            out_shape=out_shape,
            scratch_shapes=list(scratch),
            input_output_aliases=aliases or {},
            cost_estimate=pl.CostEstimate(
                flops=int(flops * share),
                bytes_accessed=int(moved * share),
                transcendentals=int(exps * share),
            ),
            compiler_params=pltpu.CompilerParams(vmem_limit_bytes=60 * 1024 * 1024),
        )(*operands)

    return run


def shape(dims, dtype):
    return jax.ShapeDtypeStruct(dims, dtype)


def whole(dims):
    return pl.BlockSpec(dims, lambda *_: (0,) * len(dims))


def each_piece(total, block, body):
    for start in range(0, total, block):
        body(pl.ds(start, block))


def fetches(pairs, sems):
    return [pltpu.make_async_copy(src, dst, sems.at[n]) for n, (src, dst) in enumerate(pairs)]


def rope(value, cosine, sine, lane):
    half = HEAD_DIM // 2
    lanes = value.shape[-1]
    swapped = jnp.where(
        lane % HEAD_DIM < half,
        pltpu.roll(value, lanes - half, 1),
        pltpu.roll(value, half, 1),
    )
    return value * cosine + swapped * sine


def qkv_kernel(own_blocks, places, me_ref, own_ref, par_ref, *refs):
    piece_refs = refs[: len(places)]
    cos_ref, sin_ref, eq_ref, ek_ref, q_ref, k_ref, v_ref, w_ref, turned_ref = refs[len(places) :]

    @pl.when(pl.program_id(0) == 0)
    def _():
        for piece_ref, (starts, column) in zip(piece_refs, places):
            _, depth, width = piece_ref.shape
            for n, start in enumerate(starts):
                row = pl.multiple_of((start ^ me_ref[0]) * depth, depth)
                w_ref[pl.ds(row, depth), column : column + width] = piece_ref[n]

    rows = jnp.where(pl.program_id(0) < own_blocks, own_ref[...], par_ref[...])
    turned_ref[...] = rows.T
    lane = lax.broadcasted_iota(jnp.int32, (rows.shape[0], SLOT), 1)
    low = lane < HEAD_DIM
    ones = jnp.where((lane >= HEAD_DIM) & (lane < HEAD_DIM + 3), -1.0, 0.0)
    cosine, sine = cos_ref[...], sin_ref[...]
    ext_q, ext_k = eq_ref[...].astype(f32), ek_ref[...].astype(f32)
    for pair in range(q_ref.shape[0] // 2):
        base = pair * 3 * SLOT
        mixed = dot(rows, w_ref[:, base : base + 3 * SLOT])
        query = rope(mixed[:, :SLOT], cosine, sine, lane) * HEAD_DIM**-0.5
        key = rope(mixed[:, SLOT : 2 * SLOT], cosine, sine, lane)
        value = mixed[:, 2 * SLOT :]
        for ref, data, ext in ((q_ref, query, ext_q), (k_ref, key, ext_k), (v_ref, value, ones)):
            ref[2 * pair] = jnp.where(low, data, ext).astype(bf16)
            ref[2 * pair + 1] = jnp.where(low, pltpu.roll(data, HEAD_DIM, 1), ext).astype(bf16)


def project_qkv(me, own, par, pieces, cosine, sine, ext_q, ext_k, block=512):
    rows, width = own.shape
    arrays = [piece[0] for piece in pieces]
    places = [piece[1:] for piece in pieces]
    columns = max(column + array.shape[2] for array, _, column in pieces)
    heads = columns // (3 * HEAD_DIM)
    count = rows // block
    table = pl.BlockSpec((block, SLOT), lambda i: (i, 0))
    out = pl.BlockSpec((heads, block, SLOT), lambda i: (0, i, 0))
    return call(
        functools.partial(qkv_kernel, count, places),
        "project_qkv",
        (2 * count,),
        [
            pl.BlockSpec(memory_space=pltpu.SMEM),
            pl.BlockSpec((block, width), lambda i: (jnp.minimum(i, count - 1), 0)),
            pl.BlockSpec((block, width), lambda i: (jnp.maximum(i - count, 0), 0)),
            *(whole(array.shape) for array in arrays),
            table,
            table,
            table,
            table,
        ],
        [out] * 3 + [whole((width, columns)), pl.BlockSpec((width, block), lambda i: (0, i))],
        [shape((heads, 2 * rows, SLOT), bf16)] * 3
        + [shape((width, columns), bf16), shape((width, 2 * rows), bf16)],
        4 * rows * width * columns,
    )(me, own, par, *arrays, cosine, sine, ext_q, ext_k)


def split_three(value):
    first = value.astype(bf16).astype(f32)
    second = (value - first).astype(bf16).astype(f32)
    return first, second, value - first - second


def attend_kernel(block, q_ref, k_ref, v_ref, ctx_ref, mix_ref, q2_ref):
    lane = lax.broadcasted_iota(jnp.int32, (block, SLOT), 1)
    low = lane < HEAD_DIM
    for piece in range(q_ref.shape[1] // block):
        rows = pl.ds(piece * block, block)
        mixed = []
        for head in range(2):
            query = q_ref[head, rows, :]
            scores = dot(query, k_ref[head], NT)
            peak = jnp.max(scores, axis=-1, keepdims=True)
            expo = jnp.exp(scores - peak).astype(bf16)
            total_mix = dot(expo, v_ref[head])
            total = -total_mix[:, HEAD_DIM : HEAD_DIM + 1]
            mixed.append(total_mix * (1.0 / total))
            parts = split_three(peak + jnp.log(total))
            kept = query.astype(f32)
            for at, part in enumerate(parts):
                kept = jnp.where(lane == HEAD_DIM + 32 + at, part, kept)
            q2_ref[head, rows, :] = kept.astype(bf16)
        both = jnp.where(low, mixed[0], pltpu.roll(mixed[1], HEAD_DIM, 1))
        mix_ref[rows, :] = both
        ctx_ref[rows, :] = both.astype(bf16)


def attend(query, keys, values, block=512, step=1024):
    heads, rows, _ = query.shape
    piece = pl.BlockSpec((2, step, SLOT), lambda p, i: (p, i, 0))
    full = pl.BlockSpec((2, rows, SLOT), lambda p, i: (p, 0, 0))
    out = pl.BlockSpec((step, SLOT), lambda p, i: (i, p))
    width = heads * HEAD_DIM
    return call(
        functools.partial(attend_kernel, block),
        "attend",
        (heads // 2, rows // step),
        [piece, full, full],
        [out, out, piece],
        [shape((rows, width), bf16), shape((rows, width), f32), shape(query.shape, bf16)],
        4 * heads * rows * rows * SLOT,
        exps=heads * rows * rows,
    )(query, keys, values)


def attend_back_kernel(
    unroll, q_ref, k_ref, v_ref, own_ref, par_ref, mix_ref, cos_ref, sin_ref, out_ref, dq_ref, dk_ref, dv_ref
):
    at = pl.program_id(1)
    block, rows = q_ref.shape[1], k_ref.shape[1]
    lane = lax.broadcasted_iota(jnp.int32, (block, SLOT), 1)
    low = lane < HEAD_DIM
    place = pl.ds(pl.multiple_of(at * block, block), block)

    @pl.when(at == 0)
    def _():
        dk_ref[...] = jnp.zeros_like(dk_ref)
        dv_ref[...] = jnp.zeros_like(dv_ref)

    def head_back(head, carry):
        first = at * 2 < pl.num_programs(1)
        grad = jnp.where(first, own_ref[...], par_ref[...]).astype(f32)
        mine = low == (head == 0)
        delta = jnp.sum(jnp.where(mine, grad * mix_ref[...], 0.0), axis=-1, keepdims=True)
        kept = jnp.where(head == 0, grad, pltpu.roll(grad, HEAD_DIM, 1))
        kept = jnp.where(low, kept, 0.0)
        for n, piece in enumerate(split_three(delta)):
            kept = jnp.where(lane == HEAD_DIM + n, piece, kept)
        grad = kept.astype(bf16)
        query, keys = q_ref[head], k_ref[head]
        probs = jnp.exp(dot(query, keys, NT))
        grad_scores = (probs * dot(grad, v_ref[head], NT)).astype(bf16)
        dv_ref[head] += dot(grad.T, probs.astype(bf16))
        dk_ref[head] += dot(query.T, grad_scores)
        dq_ref[head] = dot(grad_scores, keys)
        return carry

    lax.fori_loop(0, 2, head_back, 0, unroll=unroll)
    grad_query = jnp.where(low, dq_ref[0], pltpu.roll(dq_ref[1], HEAD_DIM, 1))
    turned = rope(grad_query, cos_ref[place, :], -sin_ref[place, :], lane)
    out_ref[place, :SLOT] = (turned * HEAD_DIM**-0.5).astype(bf16)

    @pl.when(at == pl.num_programs(1) - 1)
    def _():
        def write(n, carry):
            span = pl.ds(pl.multiple_of(n * block, block), block)
            grad_key, grad_value = (
                jnp.where(low, ref[0, :, span].T, pltpu.roll(ref[1, :, span].T, HEAD_DIM, 1))
                for ref in (dk_ref, dv_ref)
            )
            grad_key = rope(grad_key, cos_ref[span, :], -sin_ref[span, :], lane)
            out_ref[span, SLOT : 2 * SLOT] = grad_key.astype(bf16)
            out_ref[span, 2 * SLOT :] = grad_value.astype(bf16)
            return carry

        lax.fori_loop(0, rows // block, write, 0)


def attend_back(first, pairs, query, keys, values, own, par, mixed, cosine, sine, block=512, unroll=True):
    heads, rows, _ = query.shape
    half = own.shape[0]
    count = half // block
    full = pl.BlockSpec((2, rows, SLOT), lambda p, i: (first + p, 0, 0))
    return call(
        functools.partial(attend_back_kernel, unroll),
        "attend_back",
        (pairs, rows // block),
        [
            pl.BlockSpec((2, block, SLOT), lambda p, i: (first + p, i, 0)),
            full,
            full,
            pl.BlockSpec((block, SLOT), lambda p, i: (jnp.minimum(i, count - 1), first + p)),
            pl.BlockSpec((block, SLOT), lambda p, i: (jnp.maximum(i - count, 0), first + p)),
            pl.BlockSpec((block, SLOT), lambda p, i: (i, first + p)),
            whole((rows, SLOT)),
            whole((rows, SLOT)),
        ],
        pl.BlockSpec((rows, 3 * SLOT), lambda p, i: (0, p)),
        shape((rows, pairs * 3 * SLOT), bf16),
        10 * 2 * pairs * rows * rows * SLOT,
        scratch=[pltpu.VMEM((2, block, SLOT), f32)] + [pltpu.VMEM((2, SLOT, rows), f32)] * 2,
        exps=2 * pairs * rows * rows,
    )(query, keys, values, own, par, mixed, cosine, sine)


def normalize(value):
    mean = jnp.mean(value, axis=-1, keepdims=True)
    centred = value - mean
    inverse = lax.rsqrt(jnp.mean(centred * centred, axis=-1, keepdims=True) + EPS)
    return centred * inverse, inverse


def normalize_back(grad, xhat, inverse, gain):
    scaled = grad * gain
    return inverse * (
        scaled
        - jnp.mean(scaled, axis=-1, keepdims=True)
        - xhat * jnp.mean(scaled * xhat, axis=-1, keepdims=True)
    )


def fold_rows(value):
    return jnp.sum(value.reshape(-1, 8, value.shape[-1]), axis=0)


def attention_out_kernel(
    ctx_ref, got_ref, mine_ref, other_ref, tok_ref, gain_ref, xhat_ref, inv_ref, low_ref, turned_ref
):
    branch = dot(ctx_ref[...], mine_ref[...], NT) + dot(got_ref[...], other_ref[...], NT)
    xhat, inverse = normalize(tok_ref[...].astype(f32) + branch)
    xhat_ref[...] = xhat
    inv_ref[...] = inverse
    low = (xhat * gain_ref[...]).astype(bf16)
    low_ref[...] = low
    turned_ref[...] = low.T


def attention_out(ctx, got, mine, other, at, tokens, gain, block=256):
    rows, width = tokens.shape
    half = got.shape[1]
    piece = pl.BlockSpec((block, half), lambda i: (i, 0))
    row = pl.BlockSpec((block, width), lambda i: (i, 0))
    return call(
        attention_out_kernel,
        "attention_out",
        (rows // block,),
        [
            piece,
            piece,
            pl.BlockSpec((width, half), lambda i: (0, at // half)),
            whole(other.shape),
            row,
            whole((1, width)),
        ],
        [
            row,
            pl.BlockSpec((block, 1), lambda i: (i, 0)),
            row,
            pl.BlockSpec((width, block), lambda i: (0, i)),
        ],
        [
            shape((rows, width), f32),
            shape((rows, 1), f32),
            shape((rows, width), bf16),
            shape((width, rows), bf16),
        ],
        4 * rows * width * half,
    )(ctx, got, mine, other, tokens, gain)


def gate_up_tile(x_ref, gate_ref, up_ref, down_ref, act_ref, da_ref, db_ref, acc_ref, block):
    def body(span):
        gate = dot(x_ref[span, :], gate_ref[...])
        up = dot(x_ref[span, :], up_ref[...])
        sigma = jax.nn.sigmoid(gate)
        swish = gate * sigma
        act = (swish * up).astype(bf16)
        act_ref[span, :] = act
        da_ref[span, :] = (up * (sigma * (1.0 + gate * (1.0 - sigma)))).astype(bf16)
        db_ref[span, :] = swish.astype(bf16)
        acc_ref[span, :] += dot(act, down_ref[...], NT)

    each_piece(x_ref.shape[0], block, body)


def forward_first_kernel(block, x_ref, gate_ref, up_ref, down_ref, act_ref, da_ref, db_ref, acc_ref):
    @pl.when(pl.program_id(0) == 0)
    def _():
        acc_ref[...] = jnp.zeros_like(acc_ref)

    gate_up_tile(
        x_ref, gate_ref, up_ref, down_ref, act_ref, da_ref, db_ref, acc_ref, block
    )


def forward_first(x, weights, units, tile=512, block=1024):
    rows, width = x.shape
    count = units // tile
    out = pl.BlockSpec((rows, tile), lambda n: (0, n))
    return call(
        functools.partial(forward_first_kernel, block),
        "forward_first",
        (count,),
        [whole((rows, width))]
        + [pl.BlockSpec((width, tile), lambda n, at=at: (0, at * count + n)) for at in range(3)],
        [out] * 3 + [whole((rows, width))],
        [shape((rows, units), bf16)] * 3 + [shape((rows, width), f32)],
        6 * rows * width * units,
    )(x, weights, weights, weights)


def turn_kernel(
    block,
    count,
    x_ref,
    gate_w_ref,
    up_w_ref,
    down_w_ref,
    gain_a_ref,
    gain_f_ref,
    part_src,
    xhat_src,
    cot_src,
    xt_src,
    out_ref,
    mid_ref,
    low_ref,
    turned_ref,
    sum_ref,
    grads_ref,
    act_ref,
    da_ref,
    db_ref,
    grad_ref,
    acc_ref,
    part_ref,
    xhat_ref,
    cot_ref,
    xt_ref,
    sems,
):
    at = pl.program_id(0)
    copies = fetches(
        [(part_src, part_ref), (xhat_src, xhat_ref), (cot_src, cot_ref), (xt_src, xt_ref)], sems
    )

    @pl.when(at == 0)
    def _():
        acc_ref[...] = jnp.zeros_like(acc_ref)
        for copy in copies:
            copy.start()

    @pl.when(at < count)
    def _():
        gate_up_tile(
            x_ref,
            gate_w_ref,
            up_w_ref,
            down_w_ref,
            act_ref.at[at],
            da_ref.at[at],
            db_ref.at[at],
            acc_ref,
            block,
        )

    @pl.when(at == count - 1)
    def _():
        for copy in copies:
            copy.wait()
        gain_a, gain_f = gain_a_ref[...], gain_f_ref[...]
        sum_ref[...] = jnp.zeros_like(sum_ref)

        def body(span):
            branch = part_ref[span, :] + acc_ref[span, :]
            xhat, inverse = normalize(xhat_ref[span, :] * gain_a + branch)
            out_ref[span, :] = (xhat * gain_f).astype(bf16)
            grad = cot_ref[span, :].astype(f32)
            middle = normalize_back(grad, xhat, inverse, gain_f)
            mid_ref[span, :] = middle
            low = middle.astype(bf16)
            low_ref[span, :] = low
            turned_ref[:, span] = low.T
            sum_ref[...] += fold_rows(grad * xhat)

        each_piece(x_ref.shape[0], 256, body)

    @pl.when(at >= count)
    def _():
        tile = at - count

        def body(span):
            grad = dot(low_ref[span, :], down_w_ref[...])
            gate = (grad * da_ref[tile, span, :].astype(f32)).astype(bf16)
            up = (grad * db_ref[tile, span, :].astype(f32)).astype(bf16)
            grad_ref[0, span, :] = gate
            grad_ref[1, span, :] = up
            mid_ref[span, :] += dot(gate, gate_w_ref[...], NT) + dot(up, up_w_ref[...], NT)

        each_piece(x_ref.shape[0], 512, body)
        grads_ref[0] = dot(xt_ref[...], grad_ref[0]).astype(bf16)
        grads_ref[1] = dot(xt_ref[...], grad_ref[1]).astype(bf16)
        grads_ref[2] = dot(turned_ref[...], act_ref[tile]).astype(bf16)


def forward_and_back(x, turned, weights, units, part, xhat, cotangent, gain_a, gain_f, tile=512, block=1024):
    rows, width = x.shape
    count = units // tile
    full, gain = whole((rows, width)), whole((1, width))
    flat = whole((width, rows))

    def weight(part):
        return pl.BlockSpec((width, tile), lambda n: (0, part * count + lax.rem(n, count)))

    return call(
        functools.partial(turn_kernel, block, count),
        "forward_and_back",
        (2 * count,),
        [full, weight(0), weight(1), weight(2), gain, gain] + [pl.BlockSpec(memory_space=pl.ANY)] * 4,
        [
            full,
            full,
            full,
            flat,
            whole((8, width)),
            pl.BlockSpec((3, width, tile), lambda n: (0, 0, jnp.maximum(n - count, 0))),
        ],
        [
            shape((rows, width), bf16),
            shape((rows, width), f32),
            shape((rows, width), bf16),
            shape((width, rows), bf16),
            shape((8, width), f32),
            shape((3, width, units), bf16),
        ],
        18 * rows * width * units,
        scratch=[pltpu.VMEM((count, rows, tile), bf16)] * 3
        + [pltpu.VMEM((2, rows, tile), bf16)]
        + [pltpu.VMEM((rows, width), f32)] * 3
        + [
            pltpu.VMEM((rows, width), bf16),
            pltpu.VMEM((width, rows), bf16),
            pltpu.SemaphoreType.DMA((4,)),
        ],
    )(x, weights, weights, weights, gain_a, gain_f, part, xhat, cotangent, turned)


def backward_kernel(
    block,
    g_ref,
    gate_w_ref,
    up_w_ref,
    down_w_ref,
    da_ref,
    db_ref,
    part_src,
    xhat_src,
    inv_ref,
    gain_ref,
    mine_ref,
    other_ref,
    gate_ref,
    up_ref,
    res_ref,
    turned_ref,
    keep_ref,
    send_ref,
    sum_ref,
    acc_ref,
    part_ref,
    xhat_ref,
    sems,
):
    copies = fetches([(part_src, part_ref), (xhat_src, xhat_ref)], sems)

    @pl.when(pl.program_id(0) == 0)
    def _():
        acc_ref[...] = jnp.zeros_like(acc_ref)
        for copy in copies:
            copy.start()

    def tile(span):
        grad = dot(g_ref[span, :], down_w_ref[...])
        gate = (grad * da_ref[span, :].astype(f32)).astype(bf16)
        up = (grad * db_ref[span, :].astype(f32)).astype(bf16)
        gate_ref[span, :] = gate
        up_ref[span, :] = up
        acc_ref[span, :] += dot(gate, gate_w_ref[...], NT) + dot(up, up_w_ref[...], NT)

    each_piece(g_ref.shape[0], block, tile)

    @pl.when(pl.program_id(0) == pl.num_programs(0) - 1)
    def _():
        for copy in copies:
            copy.wait()
        gain = gain_ref[...]
        sum_ref[...] = jnp.zeros_like(sum_ref)

        def body(span):
            grad, xhat = acc_ref[span, :] + part_ref[span, :], xhat_ref[span, :]
            residual = normalize_back(grad, xhat, inv_ref[span, :], gain)
            res_ref[span, :] = residual
            low = residual.astype(bf16)
            turned_ref[:, span] = low.T
            keep_ref[span, :] = dot(low, mine_ref[...]).astype(bf16)
            send_ref[span, :] = dot(low, other_ref[...]).astype(bf16)
            sum_ref[...] += fold_rows(grad * xhat)

        each_piece(g_ref.shape[0], 256, body)


def backward(grad, weights, da, db, part, xhat, inverse, gain, out_other, at, tile=512, block=512):
    rows, width = grad.shape
    units, half = da.shape[1], out_other.shape[1]
    count = units // tile
    full = whole((rows, width))
    out = pl.BlockSpec((rows, tile), lambda n: (0, n))
    late = pl.BlockSpec(memory_space=pl.ANY)
    part_out = whole((rows, half))
    return call(
        functools.partial(backward_kernel, block),
        "backward",
        (count,),
        [
            full,
            *(pl.BlockSpec((width, tile), lambda n, p=p: (0, p * count + n)) for p in range(3)),
            out,
            out,
            late,
            late,
            whole((rows, 1)),
            whole((1, width)),
            pl.BlockSpec((width, half), lambda n: (0, at // half)),
            whole((width, half)),
        ],
        [out, out, full, whole((width, rows)), part_out, part_out, whole((8, width))],
        [shape((rows, units), bf16)] * 2
        + [
            shape((rows, width), f32),
            shape((width, rows), bf16),
            shape((rows, half), bf16),
            shape((rows, half), bf16),
            shape((8, width), f32),
        ],
        6 * rows * width * units + 4 * rows * width * half,
        scratch=[pltpu.VMEM((rows, width), f32)] * 3 + [pltpu.SemaphoreType.DMA((2,))],
    )(grad, weights, weights, weights, da, db, part, xhat, inverse, gain, weights, out_other)


def mirrored(index, count):
    bits = count.bit_length() - 1
    return sum(((index >> bit) & 1) << (bits - 1 - bit) for bit in range(bits))


def weight_grad_kernel(order, crossed, tiles, me_ref, *refs):
    *refs, out_ref = refs
    at = pl.program_id(0)
    first = 0
    for n, steps in enumerate(tiles):
        own_ref, par_ref, yo_ref, yp_ref = refs[4 * n : 4 * n + 4]

        def write(own_ref=own_ref, par_ref=par_ref, yo_ref=yo_ref, yp_ref=yp_ref):
            total = dot(own_ref[...], yo_ref[...]) + dot(par_ref[...], yp_ref[...])
            total = total.astype(bf16)
            if order is None:
                out_ref[...] = total
                return
            count = math.prod(order)
            depth = total.shape[0] // count
            for shard in range(count):
                apart = shard ^ me_ref[0]
                if crossed:
                    apart = (apart & (count - 4)) | ((apart & 1) << 1) | ((apart >> 1) & 1)
                out_ref[mirrored(apart, count)] = total[shard * depth : (shard + 1) * depth]

        pl.when((at >= first) & (at < first + steps))(write)
        first += steps


def weight_grad(order, me, segments, tile, crossed=False):
    rows = segments[0][2].shape[0] // 2
    width = segments[0][0][0].shape[0]
    tiles = [n // tile for *_, n in segments]
    columns = sum(tiles) * tile
    operands, specs = [me], [pl.BlockSpec(memory_space=pltpu.SMEM)]
    for n, (own, par, grad, start, _) in enumerate(segments):
        operands += [own[0], par[0], grad, grad]
        specs += [
            pl.BlockSpec((width, rows), lambda i, at=at: (0, at)) for at in (own[1], par[1])
        ]

        def column(i, first=sum(tiles[:n]), last=tiles[n] - 1, source=start // tile):
            return source + jnp.clip(i - first, 0, last)

        specs += [
            pl.BlockSpec((rows, tile), lambda i, half=half, column=column: (half, column(i)))
            for half in range(2)
        ]
    if order:
        count = math.prod(order)
        dims = (count, width // count, columns)
        out = pl.BlockSpec((*dims[:2], tile), lambda i: (0, 0, i))
    else:
        dims = (width, columns)
        out = pl.BlockSpec((width, tile), lambda i: (0, i))
    return call(
        functools.partial(weight_grad_kernel, order, crossed, tiles),
        "weight_grad",
        (sum(tiles),),
        specs,
        out,
        shape(dims, bf16),
        4 * rows * width * columns,
    )(*operands)


def dense_grad_kernel(outer, inner, tiles, add, hi_ref, *refs):
    segments = len(tiles)
    row_refs, grad_refs, refs = refs[:segments], refs[segments : 2 * segments], refs[2 * segments :]
    out_ref = refs[-1]
    at = pl.program_id(0)
    first = 0
    for row_ref, grad_ref, count in zip(row_refs, grad_refs, tiles):

        def write(row_ref=row_ref, grad_ref=grad_ref):
            total = dot(row_ref[...], grad_ref[...])
            if add:
                total = total + refs[0][0].astype(f32)
            total = total.astype(bf16)
            if outer is None:
                out_ref[...] = total
            else:
                depth = total.shape[0] // (outer * inner)
                for hi in range(outer):
                    place = hi
                    for lo in range(inner):
                        start = (hi * inner + lo) * depth
                        out_ref[lo, place] = total[start : start + depth]

        pl.when((at >= first) & (at < first + count))(write)
        first += count


def dense_grad(me_hi, segments, tile, split=None, add=None):
    width, rows = segments[0][0].shape
    tiles = [columns // tile for *_, columns in segments]
    columns = sum(tiles) * tile
    starts = [sum(tiles[:n]) for n in range(len(tiles))]

    def spec(at, start, count):
        return pl.BlockSpec((rows, tile), lambda i: (0, at // tile + jnp.clip(i - start, 0, count - 1)))

    operands = [me_hi] + [x for x, *_ in segments] + [y for _, y, *_ in segments]
    specs = [pl.BlockSpec(memory_space=pltpu.SMEM)] + [whole((width, rows)) for _ in segments]
    specs += [spec(at, start, n) for (_, _, at, _), start, n in zip(segments, starts, tiles)]
    flat = pl.BlockSpec((width, tile), lambda i: (0, i))
    if add is not None:
        operands.append(add)
        per = add.shape[2] // tile
        specs.append(pl.BlockSpec((1, width, tile), lambda i: (i // per, 0, lax.rem(i, per))))
    outer, inner = split if split else (None, None)
    if split:
        dims = (inner, outer, width // (outer * inner), columns)
        out = pl.BlockSpec((*dims[:3], tile), lambda i: (0, 0, 0, i))
    else:
        dims, out = (width, columns), flat
    return call(
        functools.partial(dense_grad_kernel, outer, inner, tiles, add is not None),
        "dense_grad",
        (columns // tile,),
        specs,
        out,
        shape(dims, bf16),
        2 * rows * width * columns,
    )(*operands)


def input_back_kernel(*refs):
    *piece_refs, w_ref, out_ref = refs
    joined = jnp.concatenate([ref[...] for ref in piece_refs], axis=1)
    out_ref[...] = dot(joined, w_ref[...], NT).astype(bf16)


def input_back_add_kernel(*refs):
    *piece_refs, w_ref, res_ref, got_ref, out_ref = refs
    joined = jnp.concatenate([ref[...] for ref in piece_refs], axis=1)
    total = dot(joined, w_ref[...], NT) + res_ref[...] + got_ref[...].astype(f32)
    out_ref[...] = total.astype(bf16)


def input_back(pieces, weights, lower, extra=(), block=256):
    rows = pieces[0].shape[0] // 2
    width, columns = weights.shape
    count = rows // block
    first = count if lower else 0
    row = pl.BlockSpec((block, width), lambda i: (i, 0))
    return call(
        input_back_add_kernel if extra else input_back_kernel,
        "input_back",
        (count,),
        [pl.BlockSpec((block, p.shape[1]), lambda i: (first + i, 0)) for p in pieces]
        + [whole(weights.shape)]
        + [row] * len(extra),
        row,
        shape((rows, width), bf16),
        2 * rows * width * columns,
    )(*pieces, weights, *extra)


def swap(value):
    return lax.ppermute(value, "mp", [(0, 1), (1, 0)])


def sum_everywhere(value, axes):
    for axis, size in axes:
        if size & (size - 1):
            return lax.psum(value, tuple(name for name, _ in axes))
    for axis, size in axes:
        step = 1
        while step < size:
            value = value + lax.ppermute(value, axis, [(i, i ^ step) for i in range(size)])
            step *= 2
    return value


def exchange(value, axis, size, step):
    return lax.ppermute(value, axis, [(i, i ^ step) for i in range(size)])


def gather_rows(shard):
    return lax.all_gather(shard, ("hi", "lo"), axis=0, tiled=True)


def gather_pieces(shard, split):
    outer, inner = split
    held = shard[None]
    step = outer // 2
    starts = [0]
    while step:
        held = jnp.concatenate([held, exchange(held, "hi", outer, step)])
        starts = starts + [start ^ (step * inner) for start in starts]
        step //= 2
    cut = shard.shape[1] // (2 * SLOT) * SLOT
    pieces = [(held, starts, 0)]
    for column, width, bits in ((0, cut, (1, 2)), (cut, shard.shape[1] - cut, (2, 1))):
        part = lax.slice_in_dim(held, column, column + width, axis=2)
        once = exchange(part, "lo", inner, bits[0])
        twice = exchange(jnp.concatenate([part, once]), "lo", inner, bits[1])
        beside = [start ^ bits[0] for start in starts]
        pieces.append((once, beside, column))
        pieces.append((twice, [start ^ bits[1] for start in starts + beside], column))
    return pieces


def scatter_first(partial, split):
    if not split:
        return lax.psum_scatter(partial, ("hi", "lo"), scatter_dimension=0, tiled=True)
    return lax.psum_scatter(partial, "lo", scatter_dimension=0, tiled=False)


def to_terms(value, columns):
    terms = jnp.stack([term.astype(bf16) for term in split_three(value)])
    whole_rows = 8 * columns
    flat = terms.reshape(-1)
    return jnp.pad(flat, (0, -flat.size % whole_rows)).reshape(-1, columns)


def from_terms(rows, dims):
    count = 3 * math.prod(dims)
    return jnp.sum(rows.reshape(-1)[:count].reshape(3, *dims).astype(f32), axis=0)


def send_half(partial, axis, size, step, rider=None):
    half, (depth, columns) = partial.shape[0] // 2, partial.shape[1:]
    message = partial[half:].reshape(half * depth, columns)
    terms = None
    if rider is not None:
        terms = to_terms(rider, columns)
        message = jnp.concatenate([message, terms])
        rider = from_terms(terms, rider.shape)
    return exchange(message, axis, size, step), (partial[:half], rider)


def take_half(got, held):
    kept, rider = held
    rows = kept.shape[0] * kept.shape[1]
    if rider is not None:
        rider = rider + from_terms(got[rows:], rider.shape)
        got = got[:rows]
    return (kept.astype(f32) + got.reshape(kept.shape).astype(f32)).astype(bf16), rider


def tie(*values):
    return lax.optimization_barrier(values)


def row_tables(block_seq, block_len, core):
    blocks = SEQ_MAX // QLEN
    sequence, lengths = block_seq.reshape(blocks), block_len.reshape(blocks)
    index = jnp.arange(blocks, dtype=jnp.int32)
    same = sequence[:, None] == sequence[None, :]
    first = jnp.min(jnp.where(same, index[None, :], blocks), axis=1)
    table = jnp.stack([sequence, lengths, QLEN * (index - first)])
    turned = jnp.concatenate([table[:, blocks // 2 :], table[:, : blocks // 2]], axis=1)
    table = jnp.where(core == 0, table, turned)
    sequence, lengths, start = (jnp.repeat(part, QLEN)[:, None] for part in table)
    inside = (jnp.arange(SEQ_MAX, dtype=jnp.int32) % QLEN)[:, None]
    position = (start + inside).astype(f32)
    valid = inside < lengths

    lane = jnp.arange(SLOT, dtype=jnp.int32)
    half = HEAD_DIM // 2
    inverse = jnp.exp((lane % half).astype(f32) * (-2.0 * math.log(ROPE_BASE) / HEAD_DIM))
    angle = position * inverse[None, :]
    cosine = jnp.cos(angle)
    sine = jnp.sin(angle) * jnp.where(lane % HEAD_DIM < half, -1.0, 1.0)[None, :]

    column = (lane - HEAD_DIM)[None, :]
    in_mask = (column >= 0) & (column < blocks)
    match = column == sequence
    ext_q = jnp.where(in_mask & match, 1.0, 0.0).astype(bf16)
    ext_k = jnp.where(
        in_mask,
        jnp.where(match & valid, 0.0, MASKED),
        jnp.where((column >= 32) & (column < 35), -1.0, 0.0),
    ).astype(bf16)
    return cosine, sine, ext_q, ext_k


def local(
    split,
    axes,
    tokens,
    w_query,
    w_key,
    w_value,
    w_out,
    w_gate,
    w_up,
    w_down,
    attention_norm_gain,
    feedforward_norm_gain,
    block_seq,
    block_len,
    cotangent,
):
    depth, units = w_gate.shape
    mine = w_query.shape[1]
    pairs = mine // SLOT
    gain_a, gain_f = attention_norm_gain[None, :], feedforward_norm_gain[None, :]

    outer, inner = split if split else (0, 0)
    me = (lax.axis_index("hi") * lax.axis_size("lo") + lax.axis_index("lo"))[None].astype(jnp.int32)
    tokens_par = swap(tokens)
    qkv_shard = jnp.concatenate(
        [
            w[:, p * SLOT : (p + 1) * SLOT]
            for p in range(pairs)
            for w in (w_query, w_key, w_value)
        ],
        axis=1,
    )
    at_up, at_down, at_out = units, 2 * units, 3 * units
    columns = at_out + mine
    w_rest = gather_rows(jnp.concatenate([w_gate, w_up, w_down.T, w_out.T], axis=1))
    if split:
        pieces = gather_pieces(qkv_shard, split)
    else:
        pieces = [(gather_rows(qkv_shard)[None], [0], 0)]
    cosine, sine, ext_q, ext_k = row_tables(block_seq, block_len, lax.axis_index("mp"))

    query, keys, values, w_qkv, tokens_t = project_qkv(
        me if split else me * 0, tokens, tokens_par, pieces, cosine, sine, ext_q, ext_k
    )
    context, mixed, query = attend(query, keys, values)
    rows = tokens.shape[0]
    context_got = swap(context[rows:])
    w_rest, context_got = tie(w_rest, context_got)
    out_other, w_rest = tie(swap(w_rest[:, at_out:]), w_rest)
    w_other = swap(w_rest)
    xhat_a, inverse_a, hidden, hidden_t = attention_out(
        context, context_got, w_rest, out_other, at_out, tokens, gain_a
    )
    act, da, db, branch = forward_first(hidden, w_rest, units)
    output, part, grad_branch, grad_branch_t, sum_f, sent = forward_and_back(
        hidden, hidden_t, w_other, units, branch, xhat_a, cotangent, gain_a, gain_f
    )

    got = swap(sent)
    grad_gate, grad_up, residual, grad_attn_t, grad_context, grad_context_send, sum_a = backward(
        grad_branch, w_rest, da, db, part, xhat_a, inverse_a, gain_a, out_other, at_out
    )
    grad_context_par = swap(grad_context_send)
    grad_attn_par = swap(grad_attn_t)
    tile = 768 if units % 768 == 0 else SLOT
    grads_rest = dense_grad(
        lax.axis_index("hi")[None].astype(jnp.int32),
        [
            (hidden_t, grad_gate, 0, units),
            (hidden_t, grad_up, 0, units),
            (grad_branch_t, act, 0, units),
        ],
        tile,
        split,
        got,
    )
    order = split

    gains = jnp.stack([jnp.sum(sum_a, axis=0), jnp.sum(sum_f, axis=0)])
    gains = gains + swap(gains)
    query, grads_rest = tie(query, grads_rest)
    grad_rest = scatter_first(grads_rest, split)
    done = attend_back(
        0, pairs, query, keys, values, grad_context, grad_context_par, mixed, cosine, sine
    )
    done, grad_rest = tie(done, grad_rest)
    each = 3 * SLOT
    cut = (pairs - 1) * each
    turned = ((tokens_t, 0), (tokens_t, 1))
    if split:
        grad_rest = lax.psum_scatter(grad_rest, "hi", scatter_dimension=0, tiled=False)
    early = weight_grad(
        order,
        me,
        [
            (*turned, done, 0, cut),
            ((grad_attn_t, 0), (grad_attn_par, 0), context, 0, mine),
        ],
        each,
    )
    early, done = tie(early, done)
    if split:
        early_got, early_held = send_half(early, "lo", inner, 1, gains)
    late = weight_grad(order, me, [(*turned, done, cut, each)], each, crossed=True)
    if split:
        late, done = tie(late, done)
        late_got, late_held = send_half(late, "lo", inner, 2)
        input_par = input_back([done], w_qkv, True)
        input_par, early_got, late_got = tie(input_par, early_got, late_got)
        input_got = swap(input_par)
        early, gains = take_half(early_got, early_held)
        early_got, early_held = send_half(early, "lo", inner, 2, gains)
        late, _ = take_half(late_got, late_held)
        late_got, late_held = send_half(late, "lo", inner, 1)
        input_grad = input_back([done], w_qkv, False, (residual, input_got))
        input_grad, late_got, early_got, grad_rest = tie(input_grad, late_got, early_got, grad_rest)
        early, gains = take_half(early_got, early_held)
        late, _ = take_half(late_got, late_held)
        both = jnp.concatenate([early, late], axis=2)
        both_got, both_held = send_half(both, "hi", outer, 1, gains)
        both, gains = take_half(both_got, both_held)
        step = 2
        while step < outer:
            both, gains = take_half(*send_half(both, "hi", outer, step, gains))
            step *= 2
        both = both[0]
    else:
        gains = sum_everywhere(gains, axes)
        both = scatter_first(jnp.concatenate([early, late], axis=1), split)
        late, done = tie(late, done)
        input_got = swap(input_back([done], w_qkv, True))
        input_grad = input_back([done], w_qkv, False, (residual, input_got))
    grad_out = both[:, cut : cut + mine].astype(f32)
    grad_qkv = jnp.concatenate([both[:, :cut], both[:, cut + mine :]], axis=1)
    grad_rest = grad_rest.astype(f32)
    grad_qkv = grad_qkv.astype(f32).reshape(depth, pairs, 3, SLOT)
    grad_query, grad_key, grad_value = (
        grad_qkv[:, :, n].reshape(depth, mine) for n in range(3)
    )
    return (
        output,
        input_grad,
        grad_query,
        grad_key,
        grad_value,
        grad_out.T,
        grad_rest[:, :units],
        grad_rest[:, units : 2 * units],
        grad_rest[:, 2 * units :].T,
        gains[0],
        gains[1],
    )


def solution(mesh):
    n_dp, n_mp = mesh.shape["dp"], mesh.shape["mp"]
    inner = 4 if n_dp % 4 == 0 else 1
    outer = n_dp // inner
    fine = Mesh(mesh.devices.reshape(outer, inner, n_mp), ("hi", "lo", "mp"))
    dp = ("hi", "lo")
    rows = P(("hi", "lo", "mp"), None)
    axes = (("mp", n_mp), ("lo", inner), ("hi", outer))

    def layer(*operands):
        width = operands[0].shape[1]
        depth = width // n_dp
        doubling = n_dp & (n_dp - 1) == 0
        split = (outer, inner) if doubling and depth % 16 == 0 and outer >= 4 else None
        return jax.shard_map(
            functools.partial(local, split, axes),
            mesh=fine,
            in_specs=(
                rows,
                P(dp, "mp"),
                P(dp, "mp"),
                P(dp, "mp"),
                P("mp", dp),
                P(dp, "mp"),
                P(dp, "mp"),
                P("mp", dp),
                P(),
                P(),
                P(dp, None),
                P(dp, None),
                rows,
            ),
            out_specs=(
                rows,
                rows,
                P(dp, "mp"),
                P(dp, "mp"),
                P(dp, "mp"),
                P("mp", dp),
                P(dp, "mp"),
                P(dp, "mp"),
                P("mp", dp),
                P(),
                P(),
            ),
            check_vma=False,
        )(*operands)

    return layer
```
